1024 devices in a mesh: sec: 4 (over z_hi), row: 8 (over y), col: 32 (over z_lo, x, core).
Axes of the slice: x: 4, y: 8, z: 16 (z_hi: 4, z_lo: 4; z = z_hi * 4 + z_lo), core: 2. Of those that a mesh axis runs over, the one named last changes fastest.
Arguments:
- labels: int32 [64, 512, 512], P('col', 'row', 'sec'), may hold values 0 or 1
- jitter: float32 [2, 64, 512, 512], P(None, 'col', 'row', 'sec'), may hold values from 0.5 to 1.5
- shells: int32 [512, 512], P('row', 'sec'), may hold values from 0 to 255, as said below
Outputs:
- populations: float32 [38, 64, 512, 512], P(None, 'col', 'row', 'sec')
- spectrum: float32 [64, 256], P('col')
The draws below stay inside these ranges and needn't reach their ends.
Inputs may be any that keep to these rules, and one draw needn't show every extreme that they name: shells are radial bins of |k|: with kx' = kx for kx < 256, else kx - 512 (ky' likewise with 512), shells[kx, ky] = min(floor(sqrt(kx'^2 + ky'^2 + j)), 255), where j is 0 or 1 per wavevector (0 at k = 0); every label from 0 to 255 belongs to at least one wavevector.
All inputs are finite; a program needn't handle non-finite values. No bound on the sum of `labels` on one device may be relied on, other than what follows from the above.
Results may differ from the reference program's by a relative error of at most 0.002.
Values may be sent and summed in bfloat16 or wider, within the bound.
A program may use at most 32 MiB of HBM per device.

```python
import math
import jax
import jax.numpy as jnp
from jax import lax

NSHELL = 256
NX = 512
NY = 512
NZ = 64


def draw_shells(key, part):
    freq_x = jnp.arange(NX, dtype=jnp.int32)
    freq_y = jnp.arange(NY, dtype=jnp.int32)
    freq_x = jnp.where(freq_x < NX // 2, freq_x, freq_x - NX)
    freq_y = jnp.where(freq_y < NY // 2, freq_y, freq_y - NY)
    radius_sq = freq_x[:, None] * freq_x[:, None] + freq_y[None, :] * freq_y[None, :]
    nudge = jax.random.randint(key, (NX, NY), 0, 2, dtype=jnp.int32)
    nudge = jnp.where(radius_sq > 0, nudge, 0)
    target = radius_sq + nudge
    guess = jnp.floor(jnp.sqrt(target.astype(jnp.float32))).astype(jnp.int32)
    guess = guess - (guess * guess > target).astype(jnp.int32)
    guess = guess + ((guess + 1) * (guess + 1) <= target).astype(jnp.int32)
    return jnp.minimum(guess, NSHELL - 1).astype(jnp.int32)


def place_ends(array, own_key, least, largest):
    longest = array.shape.index(max(array.shape))
    spots = []
    for shift in (0, 1):
        where = [jax.random.randint(jax.random.fold_in(own_key, axis), (), 0, length) for axis, length in enumerate(array.shape)]
        where[longest] = (where[longest] + shift) % array.shape[longest]
        spots.append(tuple(where))
    return array.at[spots[0]].set(least).at[spots[1]].set(largest)


def shard_levels(stream_key, shape, pieces, smallest, top_value):
    level, own = 1.0, jax.random.fold_in(stream_key, 6)
    for position, parts in pieces:
        heights = jnp.exp(jax.random.uniform(jax.random.fold_in(own, position), (parts,), jnp.float32, smallest / len(pieces), top_value / len(pieces)))
        level = level * jnp.repeat(heights, shape[position] // parts).reshape([-1 if axis == position else 1 for axis in range(len(shape))])
    return level


def setup_inputs(seed: int = 0) -> dict:
    streams_of = jax.random.split(jax.random.key(seed), 4)
    labels = place_ends((jax.random.randint(streams_of[0], (NZ, NX, NY), 0, 2) < 1).astype(jnp.int32), jax.random.fold_in(streams_of[0], 1), 0, 1)
    jitter = jnp.clip(0.5 + 1.0 * jax.random.uniform(streams_of[1], (2, NZ, NX, NY), jnp.float32) ** shard_levels(streams_of[1], (2, NZ, NX, NY), ((1, 32), (2, 8), (3, 4)), -0.2, 0.2), 0.5, 1.5)
    shells = draw_shells(jax.random.fold_in(streams_of[3], 71), 0)
    return {"labels": labels, "jitter": jitter, "shells": shells}


LATTICE = ((0, 0, 0), (1, 0, 0), (-1, 0, 0), (0, 1, 0), (0, -1, 0), (0, 0, 1), (0, 0, -1),
           (1, 1, 0), (-1, -1, 0), (1, -1, 0), (-1, 1, 0), (1, 0, 1), (-1, 0, -1), (1, 0, -1), (-1, 0, 1),
           (0, 1, 1), (0, -1, -1), (0, 1, -1), (0, -1, 1))
WEIGHTS = (1.0 / 3.0,) + (1.0 / 18.0,) * 6 + (1.0 / 36.0,) * 12


def density_pair(labels, jitter):
    heavy_a = jnp.where(labels == 1, jnp.float32(1.0), jnp.float32(0.2))
    heavy_b = jnp.where(labels == 1, jnp.float32(0.2), jnp.float32(1.0))
    return jnp.stack([heavy_a * jitter[0], heavy_b * jitter[1]])


def relax_term(density, velocity, offsets, weight):
    squared = velocity[0] * velocity[0] + velocity[1] * velocity[1] + velocity[2] * velocity[2]
    projected = offsets[0] * velocity[0] + offsets[1] * velocity[1] + offsets[2] * velocity[2]
    return weight * density * (1.0 + 1.25 * (3.0 * projected + 4.5 * projected * projected - 1.5 * squared))


def reference(labels, jitter, shells):
    densities = density_pair(labels, jitter)
    zeros_field = jnp.zeros_like(densities)
    totals_axis = [zeros_field, zeros_field, zeros_field]
    for offsets, weight in zip(LATTICE[1:], WEIGHTS[1:]):
        shifted = jnp.roll(densities, (-offsets[2], -offsets[0], -offsets[1]), axis=(1, 2, 3))
        for axis_id in range(3):
            if offsets[axis_id] != 0:
                totals_axis[axis_id] = totals_axis[axis_id] + (weight * offsets[axis_id]) * shifted
    pull_terms = jnp.stack(totals_axis, axis=1)
    velocities = (-1.6 * pull_terms[1], -1.6 * pull_terms[0])
    term_list = []
    for component in range(2):
        for offsets, weight in zip(LATTICE, WEIGHTS):
            term = relax_term(densities[component], velocities[component], offsets, weight)
            term_list.append(jnp.roll(term, (offsets[2], offsets[0], offsets[1]), axis=(0, 1, 2)))
    populations = jnp.stack(term_list)

    order_b = lax.optimization_barrier((densities[0] - densities[1]).astype(jnp.bfloat16))
    rows_x = jnp.arange(NX, dtype=jnp.int32)
    angles_x = ((rows_x[:, None] * rows_x[None, :]) % NX).astype(jnp.float32) * (2.0 * math.pi / NX)
    table_x = jnp.concatenate([jnp.cos(angles_x).astype(jnp.bfloat16), (-jnp.sin(angles_x)).astype(jnp.bfloat16)], 0)
    half_step = jnp.einsum('kx,zxy->zky', table_x.astype(jnp.float32), order_b.astype(jnp.float32)).astype(jnp.bfloat16)
    half_step = lax.optimization_barrier(half_step)
    rows_y = jnp.arange(NY, dtype=jnp.int32)
    angles_y = ((rows_y[:, None] * rows_y[None, :]) % NY).astype(jnp.float32) * (2.0 * math.pi / NY)
    cos_y = jnp.cos(angles_y).astype(jnp.bfloat16)
    sin_y = jnp.sin(angles_y).astype(jnp.bfloat16)
    right_side = jnp.concatenate([jnp.concatenate([cos_y, -sin_y], 1), jnp.concatenate([sin_y, cos_y], 1)], 0)
    left_side = jnp.concatenate([half_step[:, :NX], half_step[:, NX:]], axis=2)
    transform = jnp.einsum('zkv,vw->zkw', left_side.astype(jnp.float32), right_side.astype(jnp.float32))
    real_part = transform[..., :NY]
    imag_part = transform[..., NY:]
    power_map = real_part * real_part + imag_part * imag_part
    flat_shells = shells.reshape(NX * NY)
    totals = jax.ops.segment_sum(power_map.reshape(NZ, NX * NY).T, flat_shells, num_segments=NSHELL)
    counts = jax.ops.segment_sum(jnp.ones((NX * NY,), jnp.float32), flat_shells, num_segments=NSHELL)
    spectrum = (totals / (counts[:, None] * float(NX * NY))).T
    return populations, spectrum
```

```python
import functools
import math

import jax
import jax.numpy as jnp
import ml_dtypes
import numpy as np
from jax import lax
from jax.experimental import pallas as pl
from jax.experimental.pallas import tpu as pltpu
from jax.sharding import PartitionSpec as P

NSHELL = 256
MESH = pl.DeviceIdType.MESH

LATTICE = (
    (0, 0, 0),
    (1, 0, 0),
    (-1, 0, 0),
    (0, 1, 0),
    (0, -1, 0),
    (0, 0, 1),
    (0, 0, -1),
    (1, 1, 0),
    (-1, -1, 0),
    (1, -1, 0),
    (-1, 1, 0),
    (1, 0, 1),
    (-1, 0, -1),
    (1, 0, -1),
    (-1, 0, 1),
    (0, 1, 1),
    (0, -1, -1),
    (0, 1, -1),
    (0, -1, 1),
)
WEIGHTS = (1.0 / 3.0,) + (1.0 / 18.0,) * 6 + (1.0 / 36.0,) * 12


def trig(freq, pos, full):
    turn = (freq * pos % full).astype(np.float32) * np.float32(2.0 * math.pi / full)
    return np.cos(turn), np.sin(turn)


def x_table(rows, secs, width, full):
    per = width // secs
    freq = np.arange(full // 2)[:, None]
    cos_x, sin_x = trig(freq, np.arange(full)[None, :], full)
    imag = -sin_x
    imag[0] = trig(full // 2, np.arange(full), full)[0]
    both = np.stack([cos_x, imag], 0).reshape(2, rows // 2, secs, per, full)
    both = both.transpose(1, 2, 0, 3, 4).reshape(rows // 2, secs * 2 * per, full)
    return both.astype(ml_dtypes.bfloat16)


def y_table(full):
    cos_y, sin_y = trig(np.arange(full)[:, None], np.arange(full)[None, :], full)
    return np.concatenate([cos_y, sin_y], 1).astype(ml_dtypes.bfloat16)


def density_pair(labels, jitter_0, jitter_1):
    heavy_a = jnp.where(labels == 1, jnp.float32(1.0), jnp.float32(0.2))
    heavy_b = jnp.where(labels == 1, jnp.float32(0.2), jnp.float32(1.0))
    return heavy_a * jitter_0, heavy_b * jitter_1


def exchange_kernel(
    sizes,
    labels_ref,
    jitter_ref,
    shells_ref,
    xtab_hbm,
    ytab_hbm,
    spec_ref,
    own_ref,
    low_ref,
    high_ref,
    xtab,
    ytab,
    order_buf,
    plane_buf,
    half_send,
    half_buf,
    shell_own,
    shell_pair,
    shell_next,
    shell_send,
    shell_buf,
    ymsg,
    ybuf,
    ext,
    xsend,
    xbuf,
    zbuf,
    mask_h,
    mask_l,
    row_send,
    row_buf,
    sec_send,
    sec_buf,
    tab_sem,
    p1_send,
    p1_recv,
    p2_send,
    p2_recv,
    s1_send,
    s1_recv,
    s2_send,
    s2_recv,
    y_send,
    y_recv,
    x_send,
    x_recv,
    z_send,
    z_recv,
    ar_send,
    ar_recv,
    as_send,
    as_recv,
):
    rows, secs, cols = sizes
    depth, width_x, width_y = labels_ref.shape
    full_x, full_y = width_x * rows, width_y * secs
    per = width_x // secs
    half = rows // 2
    row, sec, col = lax.axis_index("row"), lax.axis_index("sec"), lax.axis_index("col")

    def shifted(index, step, count):
        return lax.rem(index + step + count, count)

    barrier = pltpu.get_barrier_semaphore()
    for step in range(1, rows):
        pl.semaphore_signal(
            barrier, 1, device_id={"row": shifted(row, step, rows)}, device_id_type=MESH
        )
    for step in range(1, secs):
        pl.semaphore_signal(
            barrier, 1, device_id={"sec": shifted(sec, step, secs)}, device_id_type=MESH
        )
    for step in (1, -1):
        pl.semaphore_signal(
            barrier, 1, device_id={"col": shifted(col, step, cols)}, device_id_type=MESH
        )

    block = jnp.where(row < half, row, rows - 1 - row)
    xcopy = pltpu.make_async_copy(xtab_hbm.at[block], xtab, tab_sem.at[0])
    ycopy = pltpu.make_async_copy(ytab_hbm, ytab, tab_sem.at[1])
    xcopy.start()
    ycopy.start()

    rounded = []
    for plane in range(depth):
        dens_a, dens_b = density_pair(
            labels_ref[plane], jitter_ref[0, plane], jitter_ref[1, plane]
        )
        order_buf[plane] = (dens_a - dens_b).astype(jnp.bfloat16)
        rounded.append((dens_a.astype(jnp.bfloat16), dens_b.astype(jnp.bfloat16)))
    flat = jnp.concatenate(
        [rounded[plane][part] for part in range(2) for plane in range(depth)], axis=0
    )
    pick_row = lax.broadcasted_iota(jnp.int32, (8, width_y), 0)
    pick_lane = lax.broadcasted_iota(jnp.int32, (8, width_y), 1)
    near = (pick_row < 2) & (pick_lane == pick_row)
    far = (pick_row >= 6) & (pick_lane == pick_row + (width_y - 8))
    pick = jnp.where(near | far, 1.0, 0.0).astype(jnp.bfloat16)
    ymsg[...] = lax.dot_general(
        pick, flat, (((1,), (1,)), ((), ())), preferred_element_type=jnp.float32
    )
    shell_own[...] = shells_ref[...].astype(jnp.float32).astype(jnp.bfloat16)

    pl.semaphore_wait(barrier, rows + secs)

    waits = []

    def send(src, dst, ssem, rsem, target):
        copy = pltpu.make_async_remote_copy(
            src_ref=src,
            dst_ref=dst,
            send_sem=ssem,
            recv_sem=rsem,
            device_id=target,
            device_id_type=MESH,
        )
        copy.start()
        waits.append(copy)

    def arrive(dst, ssem, rsem, axis):
        pltpu.make_async_remote_copy(
            src_ref=dst,
            dst_ref=dst,
            send_sem=ssem,
            recv_sem=rsem,
            device_id=axis,
            device_id_type=MESH,
        ).wait_recv()

    for step in range(1, rows):
        target = shifted(row, step, rows)
        send(
            order_buf.at[target // half],
            plane_buf.at[row],
            p1_send.at[step - 1],
            p1_recv.at[step - 1],
            {"row": target},
        )
    for place, step in enumerate((1, -1)):
        send(
            ymsg,
            ybuf.at[place],
            y_send.at[place],
            y_recv.at[place],
            {"sec": shifted(sec, step, secs)},
        )
    mirror = rows - 1 - row
    send(shell_own, shell_pair, s1_send.at[0], s1_recv.at[0], {"row": mirror})
    next_block = lax.rem(rows - row, half)
    next_copies = [
        pltpu.make_async_remote_copy(
            src_ref=shell_own.at[pl.ds(0, 16)],
            dst_ref=shell_next,
            send_sem=s1_send.at[1 + place],
            recv_sem=s1_recv.at[1],
            device_id={"row": target},
            device_id_type=MESH,
        )
        for place, target in enumerate((next_block, rows - 1 - next_block))
    ]

    @pl.when(row >= half)
    def _():
        for copy in next_copies:
            copy.start()

    plane_buf[row] = jnp.where(row < half, order_buf[0], order_buf[1])

    arrive(shell_pair, s1_send.at[0], s1_recv.at[0], {"row": mirror})
    arrive(shell_next, s1_send.at[1], s1_recv.at[1], {"row": mirror})
    mine = shell_own[...].astype(jnp.float32)
    other = shell_pair[...].astype(jnp.float32)
    plus = jnp.where(row < half, mine, other)
    minus = jnp.where(row < half, other, mine)
    following = shell_next[...].astype(jnp.float32)[0:1]
    row_id = lax.broadcasted_iota(jnp.int32, (width_x, width_y), 0)
    minus = jnp.where(
        row_id == width_x - 1,
        jnp.broadcast_to(following, (width_x, width_y)),
        pltpu.roll(minus, width_x - 1, 0),
    )
    for target in range(secs):
        begin = width_x - per - per * target
        shell_send[target] = jnp.concatenate(
            [plus[per * target : per * target + per], minus[begin : begin + per]], axis=0
        ).astype(jnp.bfloat16)
    for step in range(1, secs):
        target = shifted(sec, step, secs)
        send(
            shell_send.at[target],
            shell_buf.at[sec],
            s2_send.at[step - 1],
            s2_recv.at[step - 1],
            {"sec": target},
        )
    shell_buf[sec] = shell_send[sec]

    for place in range(2):
        arrive(ybuf.at[place], y_send.at[place], y_recv.at[place], {"sec": sec})
    lanes = flat.shape[0]
    side = lax.broadcasted_iota(jnp.int32, (8, lanes), 0) < 4
    columns = jnp.where(side, ybuf[1], ybuf[0])
    yhalo = lax.dot_general(
        columns.T.astype(jnp.bfloat16),
        pick,
        (((1,), (0,)), ((), ())),
        preferred_element_type=jnp.float32,
    )
    for part in range(2 * depth):
        begin = part * width_x
        ext[part, 0:width_x, 0:width_y] = flat[begin : begin + width_x].astype(jnp.float32)
        ext[part, 0:width_x, width_y : 2 * width_y] = yhalo[begin : begin + width_x]
    xsend[0] = ext[:, width_x - 8 : width_x, :]
    xsend[1] = ext[:, 0:8, :]
    for place, step in enumerate((1, -1)):
        send(
            xsend.at[place],
            xbuf.at[place],
            x_send.at[place],
            x_recv.at[place],
            {"row": shifted(row, step, rows)},
        )

    xcopy.wait()
    for step in range(1, rows):
        arrive(
            plane_buf.at[shifted(row, -step, rows)],
            p1_send.at[step - 1],
            p1_recv.at[step - 1],
            {"row": row},
        )
    half_step = jnp.dot(
        xtab[...],
        plane_buf[...].reshape(full_x, width_y),
        preferred_element_type=jnp.float32,
    )
    half_send[...] = half_step.astype(jnp.bfloat16).reshape(secs, 2 * per, width_y)
    for step in range(1, secs):
        target = shifted(sec, step, secs)
        send(
            half_send.at[target],
            half_buf.at[sec],
            p2_send.at[step - 1],
            p2_recv.at[step - 1],
            {"sec": target},
        )
    half_buf[sec] = half_send[sec]

    for place in range(2):
        arrive(xbuf.at[place], x_send.at[place], x_recv.at[place], {"row": row})
    upper = lax.broadcasted_iota(jnp.int32, (2 * depth, 8, 2 * width_y), 1) < 4
    ext[:, width_x : width_x + 8, :] = jnp.where(upper, xbuf[1], xbuf[0])
    own_ref[...] = ext[...].reshape(own_ref.shape).astype(jnp.bfloat16)
    for place, step in enumerate((1, -1)):
        send(
            own_ref,
            zbuf.at[place],
            z_send.at[place],
            z_recv.at[place],
            {"col": shifted(col, step, cols)},
        )

    for step in range(1, secs):
        arrive(
            shell_buf.at[shifted(sec, -step, secs)],
            s2_send.at[step - 1],
            s2_recv.at[step - 1],
            {"sec": sec},
        )
    shell_rows = jnp.concatenate(
        [shell_buf[source].astype(jnp.float32) for source in range(secs)], axis=1
    )
    shell_h = jnp.floor(shell_rows * (1.0 / 16.0))
    shell_l = shell_rows - 16.0 * shell_h
    label = lax.broadcasted_iota(jnp.int32, (16, full_y), 0).astype(jnp.float32)
    for line in range(2 * per):
        span = slice(line * full_y, (line + 1) * full_y)
        mask_h[:, span] = jnp.where(
            jnp.broadcast_to(shell_h[line : line + 1], (16, full_y)) == label, 1.0, 0.0
        ).astype(jnp.bfloat16)
        mask_l[32:48, span] = jnp.where(
            jnp.broadcast_to(shell_l[line : line + 1], (16, full_y)) == label, 1.0, 0.0
        ).astype(jnp.bfloat16)

    ycopy.wait()
    for step in range(1, secs):
        arrive(
            half_buf.at[shifted(sec, -step, secs)],
            p2_send.at[step - 1],
            p2_recv.at[step - 1],
            {"sec": sec},
        )
    left = jnp.concatenate([half_buf[source] for source in range(secs)], axis=1)
    product = jnp.dot(left, ytab[...], preferred_element_type=jnp.float32)
    re_cos, re_sin = product[:per, :full_y], product[:per, full_y:]
    im_cos, im_sin = product[per:, :full_y], product[per:, full_y:]
    sum_re, sum_im = re_cos + im_sin, im_cos - re_sin
    dif_re, dif_im = re_cos - im_sin, im_cos + re_sin
    first = (lax.broadcasted_iota(jnp.int32, (per, full_y), 0) == 0) & (
        (block == 0) & (sec == 0)
    )
    sum_re = jnp.where(first, re_cos, sum_re)
    sum_im = jnp.where(first, re_sin, sum_im)
    dif_re = jnp.where(first, im_cos, dif_re)
    dif_im = jnp.where(first, im_sin, dif_im)
    power = (sum_re * sum_re + sum_im * sum_im, dif_re * dif_re + dif_im * dif_im)
    coarse = [value.astype(jnp.bfloat16).astype(jnp.float32) for value in power]
    fine = [value - top for value, top in zip(power, coarse)]
    for line in range(2 * per):
        span = slice(line * full_y, (line + 1) * full_y)
        sign, kx = (0, line) if line < per else (1, 2 * per - 1 - line)
        member = mask_l[32:48, span].astype(jnp.float32)
        top = jnp.broadcast_to(coarse[sign][kx : kx + 1], (16, full_y))
        rest = jnp.broadcast_to(fine[sign][kx : kx + 1], (16, full_y))
        mask_l[0:16, span] = (member * top).astype(jnp.bfloat16)
        mask_l[16:32, span] = (member * rest).astype(jnp.bfloat16)
    table = lax.dot_general(
        mask_h[...],
        mask_l[...],
        (((1,), (1,)), ((), ())),
        preferred_element_type=jnp.float32,
    )
    row_send[...] = jnp.concatenate(
        [table, jnp.zeros((16, 128 - table.shape[1]), jnp.float32)], axis=1
    )

    for step in range(1, rows):
        send(
            row_send,
            row_buf.at[row],
            ar_send.at[step - 1],
            ar_recv.at[step - 1],
            {"row": shifted(row, step, rows)},
        )
    row_buf[row] = row_send[...]

    for place in range(2):
        arrive(zbuf.at[place], z_send.at[place], z_recv.at[place], {"col": col})
    low_ref[...] = zbuf[0]
    high_ref[...] = zbuf[1]

    for step in range(1, rows):
        arrive(
            row_buf.at[shifted(row, -step, rows)],
            ar_send.at[step - 1],
            ar_recv.at[step - 1],
            {"row": row},
        )
    total_0, total_1 = row_buf[0], row_buf[half]
    for source in range(1, half):
        total_0 = total_0 + row_buf[source]
        total_1 = total_1 + row_buf[half + source]
    sec_send[...] = total_0 + pltpu.roll(total_1, 64, 1)
    for step in range(1, secs):
        send(
            sec_send,
            sec_buf.at[sec],
            as_send.at[step - 1],
            as_recv.at[step - 1],
            {"sec": shifted(sec, step, secs)},
        )
    sec_buf[sec] = sec_send[...]
    for step in range(1, secs):
        arrive(
            sec_buf.at[shifted(sec, -step, secs)],
            as_send.at[step - 1],
            as_recv.at[step - 1],
            {"sec": sec},
        )
    total = sec_buf[0]
    for source in range(1, secs):
        total = total + sec_buf[source]
    lane = lax.broadcasted_iota(jnp.int32, (16, 128), 1)
    line_id = lax.broadcasted_iota(jnp.int32, (16, 256), 0)
    here = lax.broadcasted_iota(jnp.int32, (16, 256), 1) // 16 == line_id

    def spread(value):
        value = jnp.where(lane < 16, value, 0.0)
        for shift in (16, 32, 64):
            value = value + pltpu.roll(value, shift, 1)
        value = jnp.concatenate([value, value], axis=1)
        return jnp.sum(jnp.where(here, value, 0.0), axis=0, keepdims=True)

    both = total + pltpu.roll(total, 112, 1)
    scale = spread(pltpu.roll(total, 96, 1)) * float(full_x * full_y)
    spec_ref[0:1, :] = spread(both) / scale
    spec_ref[1:2, :] = spread(pltpu.roll(both, 64, 1)) / scale

    for copy in waits:
        copy.wait_send()

    @pl.when(row >= half)
    def _():
        for copy in next_copies:
            copy.wait_send()


def exchange(labels, jitter, shells, sizes):
    rows, secs, _ = sizes
    depth, width_x, width_y = labels.shape
    per = width_x // secs
    full_x, full_y = width_x * rows, width_y * secs
    ext_rows = 2 * depth * (width_x + 8)
    bf16, f32 = jnp.bfloat16, jnp.float32
    vmem = pl.BlockSpec(memory_space=pltpu.VMEM)
    hbm = pl.BlockSpec(memory_space=pl.ANY)
    dma = pltpu.SemaphoreType.DMA
    halo = jax.ShapeDtypeStruct((ext_rows, 2 * width_y), bf16)
    return pl.pallas_call(
        functools.partial(exchange_kernel, sizes),
        out_shape=(jax.ShapeDtypeStruct((depth, NSHELL), f32), halo, halo, halo),
        in_specs=[vmem, vmem, vmem, hbm, hbm],
        out_specs=(vmem,) * 4,
        scratch_shapes=[
            pltpu.VMEM((secs * 2 * per, full_x), bf16),
            pltpu.VMEM((full_y, 2 * full_y), bf16),
            pltpu.VMEM((depth, width_x, width_y), bf16),
            pltpu.VMEM((rows, width_x, width_y), bf16),
            pltpu.VMEM((secs, 2 * per, width_y), bf16),
            pltpu.VMEM((secs, 2 * per, width_y), bf16),
            pltpu.VMEM((width_x, width_y), bf16),
            pltpu.VMEM((width_x, width_y), bf16),
            pltpu.VMEM((16, width_y), bf16),
            pltpu.VMEM((secs, 2 * per, width_y), bf16),
            pltpu.VMEM((secs, 2 * per, width_y), bf16),
            pltpu.VMEM((8, 2 * depth * width_x), f32),
            pltpu.VMEM((2, 8, 2 * depth * width_x), f32),
            pltpu.VMEM((2 * depth, width_x + 8, 2 * width_y), f32),
            pltpu.VMEM((2, 2 * depth, 8, 2 * width_y), f32),
            pltpu.VMEM((2, 2 * depth, 8, 2 * width_y), f32),
            pltpu.VMEM((2, ext_rows, 2 * width_y), bf16),
            pltpu.VMEM((16, 2 * per * full_y), bf16),
            pltpu.VMEM((48, 2 * per * full_y), bf16),
            pltpu.VMEM((16, 128), f32),
            pltpu.VMEM((rows, 16, 128), f32),
            pltpu.VMEM((16, 128), f32),
            pltpu.VMEM((secs, 16, 128), f32),
            dma((2,)),
            dma((rows - 1,)),
            dma((rows - 1,)),
            dma((secs - 1,)),
            dma((secs - 1,)),
            dma((3,)),
            dma((2,)),
            dma((secs - 1,)),
            dma((secs - 1,)),
            dma((2,)),
            dma((2,)),
            dma((2,)),
            dma((2,)),
            dma((2,)),
            dma((2,)),
            dma((rows - 1,)),
            dma((rows - 1,)),
            dma((secs - 1,)),
            dma((secs - 1,)),
        ],
        compiler_params=pltpu.CompilerParams(collective_id=0, has_side_effects=True),
        name="exchange",
    )(
        labels,
        jitter,
        shells,
        jnp.asarray(x_table(rows, secs, width_x, full_x)),
        jnp.asarray(y_table(full_y)),
    )


def stream_kernel(labels_ref, jitter_ref, own_ref, low_ref, high_ref, out_ref, field):
    part = pl.program_id(0)
    plane = pl.program_id(1)
    depth, width_x, width_y = labels_ref.shape
    rows, lanes = field.shape[2], field.shape[3]

    @pl.when((part == 0) & (plane == 0))
    def _():
        shape = (2, depth, rows, lanes)
        field[:, 0:depth] = low_ref[...].astype(jnp.float32).reshape(shape)
        field[:, depth : 2 * depth] = own_ref[...].astype(jnp.float32).reshape(shape)
        field[:, 2 * depth : 3 * depth] = high_ref[...].astype(jnp.float32).reshape(shape)
        for level in range(depth):
            pair = density_pair(labels_ref[level], jitter_ref[0, level], jitter_ref[1, level])
            for which in range(2):
                field[which, depth + level, 0:width_x, 0:width_y] = pair[which]

    def moved(value, step, axis):
        return value if step == 0 else pltpu.roll(value, step % value.shape[axis], axis)

    other = [field[1 - part, plane + level] for level in range(5)]
    around_x = [moved(value, 1, 0) + moved(value, -1, 0) for value in other]
    around_y = [moved(value, 1, 1) + moved(value, -1, 1) for value in other]
    flat_sum = [
        2.0 * other[level] + around_x[level] + around_y[level] for level in range(5)
    ]
    for shift_z in (1, 0, -1):
        level = 2 - shift_z
        between = 2.0 * other[level] + other[level + 1] + other[level - 1]
        tall_x = between + around_y[level]
        tall_y = between + around_x[level]
        gain = -1.6 / 36.0
        vel_x = gain * (moved(tall_x, -1, 0) - moved(tall_x, 1, 0))
        vel_y = gain * (moved(tall_y, -1, 1) - moved(tall_y, 1, 1))
        vel_z = gain * (flat_sum[level + 1] - flat_sum[level - 1])
        density = field[part, plane + level]
        rest = density * (
            1.0 - 1.875 * (vel_x * vel_x + vel_y * vel_y + vel_z * vel_z)
        )
        for number, (offsets, weight) in enumerate(zip(LATTICE, WEIGHTS)):
            if offsets[2] != shift_z:
                continue
            along = None
            for step, speed in zip(offsets, (vel_x, vel_y, vel_z)):
                if step != 0:
                    term = speed if step == 1 else -speed
                    along = term if along is None else along + term
            value = rest
            if along is not None:
                value = rest + density * (along * (3.75 + 5.625 * along))
            value = weight * value
            value = moved(moved(value, offsets[0], 0), offsets[1], 1)
            out_ref[number, 0] = value[0:width_x, 0:width_y]


def stream(labels, jitter, own, low, high):
    depth, width_x, width_y = labels.shape
    vmem = pl.BlockSpec(memory_space=pltpu.VMEM)
    return pl.pallas_call(
        stream_kernel,
        grid=(2, depth),
        out_shape=jax.ShapeDtypeStruct((38, depth, width_x, width_y), jnp.float32),
        in_specs=[vmem] * 5,
        out_specs=pl.BlockSpec(
            (19, 1, width_x, width_y), lambda part, plane: (part, plane, 0, 0)
        ),
        scratch_shapes=[
            pltpu.VMEM((2, 3 * depth, width_x + 8, 2 * width_y), jnp.float32)
        ],
        name="stream",
    )(labels, jitter, own, low, high)


def solution(mesh):
    sizes = tuple(mesh.shape[name] for name in ("row", "sec", "col"))

    def on_device(labels, jitter, shells):
        spectrum, own, low, high = exchange(labels, jitter, shells, sizes)
        return stream(labels, jitter, own, low, high), spectrum

    in_specs = (P("col", "row", "sec"), P(None, "col", "row", "sec"), P("row", "sec"))
    out_specs = (P(None, "col", "row", "sec"), P("col", None))
    return jax.shard_map(
        on_device, mesh=mesh, in_specs=in_specs, out_specs=out_specs, check_vma=False
    )
```

```python
import functools
import math

import jax
import jax.numpy as jnp
import ml_dtypes
import numpy as np
from jax import lax
from jax.experimental import pallas as pl
from jax.experimental.pallas import tpu as pltpu
from jax.sharding import PartitionSpec as P

NSHELL = 256
MESH = pl.DeviceIdType.MESH

LATTICE = (
    (0, 0, 0),
    (1, 0, 0),
    (-1, 0, 0),
    (0, 1, 0),
    (0, -1, 0),
    (0, 0, 1),
    (0, 0, -1),
    (1, 1, 0),
    (-1, -1, 0),
    (1, -1, 0),
    (-1, 1, 0),
    (1, 0, 1),
    (-1, 0, -1),
    (1, 0, -1),
    (-1, 0, 1),
    (0, 1, 1),
    (0, -1, -1),
    (0, 1, -1),
    (0, -1, 1),
)
WEIGHTS = (1.0 / 3.0,) + (1.0 / 18.0,) * 6 + (1.0 / 36.0,) * 12


def trig(freq, pos, full):
    turn = (freq * pos % full).astype(np.float32) * np.float32(2.0 * math.pi / full)
    return np.cos(turn), np.sin(turn)


def x_table(rows, width, full):
    cos_x, sin_x = trig(np.arange(full // 2)[:, None], np.arange(full)[None, :], full)
    imag = -sin_x
    imag[0] = trig(full // 2, np.arange(full), full)[0]
    both = np.stack([cos_x, imag], 0).reshape(2, rows // 2, width, full)
    both = both.transpose(1, 0, 2, 3).reshape(rows // 2, 2 * width, full)
    return both.astype(ml_dtypes.bfloat16)


def y_table(full):
    cos_y, sin_y = trig(np.arange(full)[:, None], np.arange(full)[None, :], full)
    return np.concatenate([cos_y, sin_y], 1).astype(ml_dtypes.bfloat16)


def density_pair(labels, jitter_0, jitter_1):
    heavy_a = jnp.where(labels == 1, jnp.float32(1.0), jnp.float32(0.2))
    heavy_b = jnp.where(labels == 1, jnp.float32(0.2), jnp.float32(1.0))
    return heavy_a * jitter_0, heavy_b * jitter_1


def populations_of(part, field, out_buf):
    _, levels, rows, lanes = field.shape
    width_x, width_y = rows - 8, lanes // 2
    depth = levels - 4
    lane = lax.broadcasted_iota(jnp.int32, (rows, width_y), 1)

    def moved(value, step, axis):
        return pltpu.roll(value, step % value.shape[axis], axis)

    def streamed(value, step_x, step_y):
        if step_y != 0:
            shift, edge = (1, 0) if step_y == 1 else (width_y - 1, width_y - 1)
            value = jnp.where(
                lane == edge,
                pltpu.roll(value[:, width_y:], shift, 1),
                pltpu.roll(value[:, :width_y], shift, 1),
            )
        if step_x != 0:
            value = moved(value, step_x, 0)
        return value[:width_x]

    other, around_x, around_y = [], [], []
    for level in range(levels):
        value = field[1 - part, level]
        other.append(value)
        around_x.append(moved(value, 1, 0) + moved(value, -1, 0))
        around_y.append(moved(value, 1, 1) + moved(value, -1, 1))
    flat_sum = [
        2.0 * other[level] + around_x[level] + around_y[level] for level in range(levels)
    ]
    gain = -1.6 / 36.0
    for level in range(1, levels - 1):
        between = 2.0 * other[level] + other[level + 1] + other[level - 1]
        tall_x = between + around_y[level]
        tall_y = between + around_x[level]
        speeds = (
            gain * (moved(tall_x, -1, 0) - moved(tall_x, 1, 0)),
            gain * (moved(tall_y, -1, 1) - moved(tall_y, 1, 1)),
            gain * (flat_sum[level + 1] - flat_sum[level - 1]),
        )
        density = field[part, level]
        squares = speeds[0] * speeds[0] + speeds[1] * speeds[1] + speeds[2] * speeds[2]
        rest = density * (1.0 - 1.875 * squares)
        scaled = {}
        for weight in sorted(set(WEIGHTS)):
            scaled[weight] = (
                weight * rest,
                (3.75 * weight) * density,
                (5.625 * weight) * density,
            )
        for number, (offsets, weight) in enumerate(zip(LATTICE, WEIGHTS)):
            target = level - 2 + offsets[2]
            if target < 0 or target >= depth:
                continue
            span = lanes if offsets[1] != 0 else width_y
            base, linear, square = (value[:, :span] for value in scaled[weight])
            along = None
            for step, speed in zip(offsets, speeds):
                if step != 0:
                    term = speed[:, :span]
                    if along is None:
                        along = term if step == 1 else -term
                    else:
                        along = along + term if step == 1 else along - term
            value = base
            if along is not None:
                value = base + along * (linear + square * along)
            out_buf[part * 19 + number, target] = streamed(value, offsets[0], offsets[1])


def exchange_kernel(
    sizes,
    labels_ref,
    jitter_ref,
    shells_ref,
    xtab_hbm,
    ytab_hbm,
    pop_hbm,
    spec_ref,
    xtab,
    ytab,
    order_buf,
    plane_buf,
    half_send,
    half_buf,
    shell_own,
    shell_pair,
    shell_next,
    shell_send,
    shell_buf,
    ymsg,
    ybuf,
    ext,
    xsend,
    xbuf,
    zsend,
    zbuf,
    field,
    out_buf,
    mask_h,
    mask_l,
    counts,
    power,
    row_send,
    row_buf,
    spec_send,
    spec_buf,
    tab_sem,
    out_sem,
    p1_send,
    p1_recv,
    p2_send,
    p2_recv,
    s1_send,
    s1_recv,
    s2_send,
    s2_recv,
    y_send,
    y_recv,
    x_send,
    x_recv,
    z_send,
    z_recv,
    ar_send,
    ar_recv,
    as_send,
    as_recv,
):
    rows, secs, cols = sizes
    depth, width_x, width_y = labels_ref.shape
    full_x, full_y = width_x * rows, width_y * secs
    half = rows // 2
    row, sec, col = lax.axis_index("row"), lax.axis_index("sec"), lax.axis_index("col")
    hub = sec == 0

    def shifted(index, step, count):
        return lax.rem(index + step + count, count)

    barrier = pltpu.get_barrier_semaphore()
    for step in range(1, rows):
        pl.semaphore_signal(
            barrier, 1, device_id={"row": shifted(row, step, rows)}, device_id_type=MESH
        )
    for step in range(1, secs):
        pl.semaphore_signal(
            barrier, 1, device_id={"sec": shifted(sec, step, secs)}, device_id_type=MESH
        )
    for step in (1, -1):
        pl.semaphore_signal(
            barrier, 1, device_id={"col": shifted(col, step, cols)}, device_id_type=MESH
        )

    block = jnp.where(row < half, row, rows - 1 - row)
    xcopy = pltpu.make_async_copy(xtab_hbm.at[block], xtab, tab_sem.at[0])
    ycopy = pltpu.make_async_copy(ytab_hbm, ytab, tab_sem.at[1])
    xcopy.start()
    ycopy.start()

    rounded = []
    for plane in range(depth):
        pair = density_pair(labels_ref[plane], jitter_ref[0, plane], jitter_ref[1, plane])
        order_buf[plane] = (pair[0] - pair[1]).astype(jnp.bfloat16)
        rounded.append([value.astype(jnp.bfloat16) for value in pair])
    flat = jnp.concatenate(
        [rounded[plane][part] for part in range(2) for plane in range(depth)], axis=0
    )
    pick_row = lax.broadcasted_iota(jnp.int32, (8, width_y), 0)
    pick_lane = lax.broadcasted_iota(jnp.int32, (8, width_y), 1)
    near = (pick_row < 2) & (pick_lane == pick_row)
    far = (pick_row >= 6) & (pick_lane == pick_row + (width_y - 8))
    pick = jnp.where(near | far, 1.0, 0.0).astype(jnp.bfloat16)
    ymsg[...] = lax.dot_general(
        pick, flat, (((1,), (1,)), ((), ())), preferred_element_type=jnp.float32
    )
    shell_own[...] = shells_ref[...].astype(jnp.float32).astype(jnp.bfloat16)

    pl.semaphore_wait(barrier, rows + secs)

    waits = []

    def transfer(src, dst, ssem, rsem, target):
        return pltpu.make_async_remote_copy(
            src_ref=src,
            dst_ref=dst,
            send_sem=ssem,
            recv_sem=rsem,
            device_id=target,
            device_id_type=MESH,
        )

    def send(src, dst, ssem, rsem, target):
        copy = transfer(src, dst, ssem, rsem, target)
        copy.start()
        waits.append(copy)

    def arrive(dst, ssem, rsem, target):
        transfer(dst, dst, ssem, rsem, target).wait_recv()

    order = sorted(range(1, rows), key=lambda step: -min(step, rows - step))
    for step in order:
        target = shifted(row, step, rows)
        send(
            order_buf.at[target // half],
            plane_buf.at[row],
            p1_send.at[step - 1],
            p1_recv.at[step - 1],
            {"row": target},
        )
    for place, step in enumerate((1, -1)):
        send(
            ymsg,
            ybuf.at[place],
            y_send.at[place],
            y_recv.at[place],
            {"sec": shifted(sec, step, secs)},
        )
    mirror = rows - 1 - row
    send(shell_own, shell_pair, s1_send.at[0], s1_recv.at[0], {"row": mirror})
    next_block = lax.rem(rows - row, half)
    next_copies = [
        transfer(
            shell_own.at[pl.ds(0, 16)],
            shell_next,
            s1_send.at[1 + place],
            s1_recv.at[1],
            {"row": target},
        )
        for place, target in enumerate((next_block, rows - 1 - next_block))
    ]

    @pl.when(row >= half)
    def _():
        for copy in next_copies:
            copy.start()

    plane_buf[row] = jnp.where(row < half, order_buf[0], order_buf[1])

    arrive(shell_pair, s1_send.at[0], s1_recv.at[0], {"row": mirror})
    arrive(shell_next, s1_send.at[1], s1_recv.at[1], {"row": mirror})
    mine = shell_own[...].astype(jnp.float32)
    paired = shell_pair[...].astype(jnp.float32)
    plus = jnp.where(row < half, mine, paired)
    minus = jnp.where(row < half, paired, mine)
    following = shell_next[...].astype(jnp.float32)[0:1]
    row_id = lax.broadcasted_iota(jnp.int32, (width_x, width_y), 0)
    minus = jnp.where(
        row_id == width_x - 1,
        jnp.broadcast_to(following, (width_x, width_y)),
        pltpu.roll(minus, width_x - 1, 0),
    )
    shell_send[...] = jnp.concatenate([plus, minus], axis=0).astype(jnp.bfloat16)
    from_sec = jnp.maximum(sec - 1, 0)
    shell_copy = transfer(
        shell_send, shell_buf.at[sec], s2_send.at[0], s2_recv.at[from_sec], {"sec": 0}
    )

    @pl.when(sec > 0)
    def _():
        shell_copy.start()

    for place in range(2):
        arrive(ybuf.at[place], y_send.at[place], y_recv.at[place], {"sec": sec})
    lanes = flat.shape[0]
    side = lax.broadcasted_iota(jnp.int32, (8, lanes), 0) < 4
    columns = jnp.where(side, ybuf[1], ybuf[0])
    yhalo = lax.dot_general(
        columns.T.astype(jnp.bfloat16),
        pick,
        (((1,), (0,)), ((), ())),
        preferred_element_type=jnp.float32,
    )
    for part in range(2 * depth):
        begin = part * width_x
        ext[part, 0:width_x, 0:width_y] = flat[begin : begin + width_x].astype(jnp.float32)
        ext[part, 0:width_x, width_y : 2 * width_y] = yhalo[begin : begin + width_x]
    xsend[0] = ext[:, width_x - 8 : width_x, :]
    xsend[1] = ext[:, 0:8, :]
    for place, step in enumerate((1, -1)):
        send(
            xsend.at[place],
            xbuf.at[place],
            x_send.at[place],
            x_recv.at[place],
            {"row": shifted(row, step, rows)},
        )

    xcopy.wait()
    for step in order:
        arrive(
            plane_buf.at[shifted(row, -step, rows)],
            p1_send.at[step - 1],
            p1_recv.at[step - 1],
            {"row": row},
        )
    half_step = jnp.dot(
        xtab[...],
        plane_buf[...].reshape(full_x, width_y),
        preferred_element_type=jnp.float32,
    )
    half_send[...] = half_step.astype(jnp.bfloat16)
    half_copy = transfer(
        half_send, half_buf.at[sec], p2_send.at[0], p2_recv.at[from_sec], {"sec": 0}
    )

    @pl.when(sec > 0)
    def _():
        half_copy.start()

    for place in range(2):
        arrive(xbuf.at[place], x_send.at[place], x_recv.at[place], {"row": row})
    upper = lax.broadcasted_iota(jnp.int32, (2 * depth, 8, 2 * width_y), 1) < 4
    ext[:, width_x : width_x + 8, :] = jnp.where(upper, xbuf[1], xbuf[0])
    zsend[...] = ext[...].reshape(zsend.shape).astype(jnp.bfloat16)
    for place, step in enumerate((1, -1)):
        send(
            zsend,
            zbuf.at[place],
            z_send.at[place],
            z_recv.at[place],
            {"col": shifted(col, step, cols)},
        )
    shape = (2, depth, width_x + 8, 2 * width_y)
    field[:, depth : 2 * depth] = ext[...].reshape(shape)
    for plane in range(depth):
        pair = density_pair(labels_ref[plane], jitter_ref[0, plane], jitter_ref[1, plane])
        for part in range(2):
            field[part, depth + plane, 0:width_x, 0:width_y] = pair[part]

    lane = lax.broadcasted_iota(jnp.int32, (16, 128), 1)
    line_id = lax.broadcasted_iota(jnp.int32, (16, 256), 0)
    here = lax.broadcasted_iota(jnp.int32, (16, 256), 1) // 16 == line_id

    def spread(value):
        value = jnp.where(lane < 16, value, 0.0)
        for shift in (16, 32, 64):
            value = value + pltpu.roll(value, shift, 1)
        value = jnp.concatenate([value, value], axis=1)
        return jnp.sum(jnp.where(here, value, 0.0), axis=0, keepdims=True)

    def widen(value):
        blank = jnp.zeros((16, 128 - value.shape[1]), jnp.float32)
        return jnp.concatenate([value, blank], axis=1)

    def contract(left, right):
        return lax.dot_general(
            left, right, (((1,), (1,)), ((), ())), preferred_element_type=jnp.float32
        )

    @pl.when(hub)
    def _():
        shell_buf[0] = shell_send[...]
        for source in range(1, secs):
            arrive(
                shell_buf.at[source],
                s2_send.at[0],
                s2_recv.at[source - 1],
                {"sec": sec},
            )
        label = lax.broadcasted_iota(jnp.int32, (16, full_y), 0).astype(jnp.float32)

        def build(step, total):
            begin = pl.multiple_of(step * 16, 16)
            value = jnp.concatenate(
                [
                    shell_buf[source, pl.ds(begin, 16), :].astype(jnp.float32)
                    for source in range(secs)
                ],
                axis=1,
            )
            upper_digit = jnp.floor(value * (1.0 / 16.0))
            lower_digit = value - 16.0 * upper_digit
            for line in range(16):
                tall = (16, full_y)
                high = jnp.where(
                    jnp.broadcast_to(upper_digit[line : line + 1], tall) == label, 1.0, 0.0
                ).astype(jnp.bfloat16)
                low = jnp.where(
                    jnp.broadcast_to(lower_digit[line : line + 1], tall) == label, 1.0, 0.0
                ).astype(jnp.bfloat16)
                mask_h[begin + line] = high
                mask_l[begin + line] = low
                total = total + contract(high, low)
            return total

        counts[...] = lax.fori_loop(
            0, 2 * width_x // 16, build, jnp.zeros((16, 16), jnp.float32)
        )

        ycopy.wait()
        half_buf[0] = half_send[...]
        for source in range(1, secs):
            arrive(
                half_buf.at[source], p2_send.at[0], p2_recv.at[source - 1], {"sec": sec}
            )
        left = jnp.concatenate([half_buf[source] for source in range(secs)], axis=1)
        product = jnp.dot(left, ytab[...], preferred_element_type=jnp.float32)
        re_cos, re_sin = product[:width_x, :full_y], product[:width_x, full_y:]
        im_cos, im_sin = product[width_x:, :full_y], product[width_x:, full_y:]
        first = (lax.broadcasted_iota(jnp.int32, (width_x, full_y), 0) == 0) & (block == 0)
        sum_re = jnp.where(first, re_cos, re_cos + im_sin)
        sum_im = jnp.where(first, re_sin, im_cos - re_sin)
        dif_re = jnp.where(first, im_cos, re_cos - im_sin)
        dif_im = jnp.where(first, im_sin, im_cos + re_sin)
        power[0] = sum_re * sum_re + sum_im * sum_im
        power[1] = dif_re * dif_re + dif_im * dif_im

        def gather(step, total):
            begin = pl.multiple_of(step * 8, 8)
            for sign in range(2):
                value = power[sign, pl.ds(begin, 8), :]
                coarse = value.astype(jnp.bfloat16).astype(jnp.float32)
                fine = value - coarse
                for line in range(8):
                    place = begin + line
                    if sign == 1:
                        place = 2 * width_x - 1 - place
                    member = mask_l[place]
                    tall = (16, full_y)
                    top = jnp.broadcast_to(coarse[line : line + 1], tall)
                    rest = jnp.broadcast_to(fine[line : line + 1], tall)
                    right = jnp.concatenate(
                        [
                            member * top.astype(jnp.bfloat16),
                            member * rest.astype(jnp.bfloat16),
                        ],
                        axis=0,
                    )
                    total = total + contract(mask_h[place], right)
            return total

        table = widen(
            lax.fori_loop(0, width_x // 8, gather, jnp.zeros((16, 32), jnp.float32))
        )
        row_send[0:1, :] = spread(table + pltpu.roll(table, 112, 1))
        row_send[1:2, :] = spread(widen(counts[...]))
        for step in order:
            transfer(
                row_send,
                row_buf.at[row],
                ar_send.at[step - 1],
                ar_recv.at[step - 1],
                {"row": shifted(row, step, rows)},
            ).start()
        row_buf[row] = row_send[...]

    for place in range(2):
        arrive(zbuf.at[place], z_send.at[place], z_recv.at[place], {"col": col})
    field[:, 0:depth] = zbuf[0].astype(jnp.float32).reshape(shape)
    field[:, 2 * depth : 3 * depth] = zbuf[1].astype(jnp.float32).reshape(shape)
    drains = [
        pltpu.make_async_copy(
            out_buf.at[pl.ds(part * 19, 19)],
            pop_hbm.at[pl.ds(part * 19, 19)],
            out_sem.at[part],
        )
        for part in range(2)
    ]
    for part in range(2):
        populations_of(part, field, out_buf)
        drains[part].start()

    @pl.when(hub)
    def _():
        for step in order:
            arrive(
                row_buf.at[shifted(row, -step, rows)],
                ar_send.at[step - 1],
                ar_recv.at[step - 1],
                {"row": row},
            )
        sums = []
        for start in (0, half):
            total = row_buf[start]
            for source in range(start + 1, start + half):
                total = total + row_buf[source]
            sums.append(total)
        scale = sums[0][1:2] * float(full_x * full_y)
        spec_send[0:1, :] = sums[0][0:1] / scale
        spec_send[1:2, :] = sums[1][0:1] / scale
        spec_copies = [
            transfer(
                spec_send, spec_buf, as_send.at[target - 1], as_recv.at[0], {"sec": target}
            )
            for target in range(1, secs)
        ]
        for copy in spec_copies:
            copy.start()
        spec_ref[...] = spec_send[...]
        for copy in spec_copies:
            copy.wait_send()
        for step in order:
            transfer(
                row_send,
                row_buf.at[row],
                ar_send.at[step - 1],
                ar_recv.at[step - 1],
                {"row": row},
            ).wait_send()

    @pl.when(sec > 0)
    def _():
        arrive(spec_buf, as_send.at[0], as_recv.at[0], {"sec": sec})
        spec_ref[...] = spec_buf[...]
        ycopy.wait()
        shell_copy.wait_send()
        half_copy.wait_send()

    for copy in waits:
        copy.wait_send()

    @pl.when(row >= half)
    def _():
        for copy in next_copies:
            copy.wait_send()

    for copy in drains:
        copy.wait()


def exchange(labels, jitter, shells, sizes):
    rows, secs, _ = sizes
    depth, width_x, width_y = labels.shape
    full_x, full_y = width_x * rows, width_y * secs
    ext_rows = 2 * depth * (width_x + 8)
    bf16, f32 = jnp.bfloat16, jnp.float32
    vmem = pl.BlockSpec(memory_space=pltpu.VMEM)
    hbm = pl.BlockSpec(memory_space=pl.ANY)
    dma = pltpu.SemaphoreType.DMA
    return pl.pallas_call(
        functools.partial(exchange_kernel, sizes),
        out_shape=(
            jax.ShapeDtypeStruct((38, depth, width_x, width_y), f32),
            jax.ShapeDtypeStruct((depth, NSHELL), f32),
        ),
        in_specs=[vmem, vmem, vmem, hbm, hbm],
        out_specs=(hbm, vmem),
        scratch_shapes=[
            pltpu.VMEM((2 * width_x, full_x), bf16),
            pltpu.VMEM((full_y, 2 * full_y), bf16),
            pltpu.VMEM((depth, width_x, width_y), bf16),
            pltpu.VMEM((rows, width_x, width_y), bf16),
            pltpu.VMEM((2 * width_x, width_y), bf16),
            pltpu.VMEM((secs, 2 * width_x, width_y), bf16),
            pltpu.VMEM((width_x, width_y), bf16),
            pltpu.VMEM((width_x, width_y), bf16),
            pltpu.VMEM((16, width_y), bf16),
            pltpu.VMEM((2 * width_x, width_y), bf16),
            pltpu.VMEM((secs, 2 * width_x, width_y), bf16),
            pltpu.VMEM((8, 2 * depth * width_x), f32),
            pltpu.VMEM((2, 8, 2 * depth * width_x), f32),
            pltpu.VMEM((2 * depth, width_x + 8, 2 * width_y), f32),
            pltpu.VMEM((2, 2 * depth, 8, 2 * width_y), f32),
            pltpu.VMEM((2, 2 * depth, 8, 2 * width_y), f32),
            pltpu.VMEM((ext_rows, 2 * width_y), bf16),
            pltpu.VMEM((2, ext_rows, 2 * width_y), bf16),
            pltpu.VMEM((2, 3 * depth, width_x + 8, 2 * width_y), f32),
            pltpu.VMEM((38, depth, width_x, width_y), f32),
            pltpu.VMEM((2 * width_x, 16, full_y), bf16),
            pltpu.VMEM((2 * width_x, 16, full_y), bf16),
            pltpu.VMEM((16, 16), f32),
            pltpu.VMEM((2, width_x, full_y), f32),
            pltpu.VMEM((2, NSHELL), f32),
            pltpu.VMEM((rows, 2, NSHELL), f32),
            pltpu.VMEM((2, NSHELL), f32),
            pltpu.VMEM((2, NSHELL), f32),
            dma((2,)),
            dma((2,)),
            dma((rows - 1,)),
            dma((rows - 1,)),
            dma((1,)),
            dma((secs - 1,)),
            dma((3,)),
            dma((2,)),
            dma((1,)),
            dma((secs - 1,)),
            dma((2,)),
            dma((2,)),
            dma((2,)),
            dma((2,)),
            dma((2,)),
            dma((2,)),
            dma((rows - 1,)),
            dma((rows - 1,)),
            dma((secs - 1,)),
            dma((1,)),
        ],
        compiler_params=pltpu.CompilerParams(collective_id=0, has_side_effects=True),
        name="exchange",
    )(
        labels,
        jitter,
        shells,
        jnp.asarray(x_table(rows, width_x, full_x)),
        jnp.asarray(y_table(full_y)),
    )


def solution(mesh):
    sizes = tuple(mesh.shape[name] for name in ("row", "sec", "col"))

    def on_device(labels, jitter, shells):
        return exchange(labels, jitter, shells, sizes)

    in_specs = (P("col", "row", "sec"), P(None, "col", "row", "sec"), P("row", "sec"))
    out_specs = (P(None, "col", "row", "sec"), P("col", None))
    return jax.shard_map(
        on_device, mesh=mesh, in_specs=in_specs, out_specs=out_specs, check_vma=False
    )
```

```python
import functools
import math

import jax
import jax.numpy as jnp
import ml_dtypes
import numpy as np
from jax import lax
from jax.experimental import pallas as pl
from jax.experimental.pallas import tpu as pltpu
from jax.sharding import PartitionSpec as P

NSHELL = 256
MESH = pl.DeviceIdType.MESH

LATTICE = (
    (0, 0, 0),
    (1, 0, 0),
    (-1, 0, 0),
    (0, 1, 0),
    (0, -1, 0),
    (0, 0, 1),
    (0, 0, -1),
    (1, 1, 0),
    (-1, -1, 0),
    (1, -1, 0),
    (-1, 1, 0),
    (1, 0, 1),
    (-1, 0, -1),
    (1, 0, -1),
    (-1, 0, 1),
    (0, 1, 1),
    (0, -1, -1),
    (0, 1, -1),
    (0, -1, 1),
)
WEIGHTS = (1.0 / 3.0,) + (1.0 / 18.0,) * 6 + (1.0 / 36.0,) * 12


def trig(freq, pos, full):
    turn = (freq * pos % full).astype(np.float32) * np.float32(2.0 * math.pi / full)
    return np.cos(turn), np.sin(turn)


def x_table(rows, width, full):
    cos_x, sin_x = trig(np.arange(full // 2)[:, None], np.arange(full)[None, :], full)
    imag = -sin_x
    imag[0] = trig(full // 2, np.arange(full), full)[0]
    both = np.stack([cos_x, imag], 0).reshape(2, rows // 2, width, full)
    both = both.transpose(1, 0, 2, 3).reshape(rows // 2, 2 * width, full)
    return both.astype(ml_dtypes.bfloat16)


def y_table(full):
    cos_y, sin_y = trig(np.arange(full)[:, None], np.arange(full)[None, :], full)
    return np.concatenate([cos_y, sin_y], 1).astype(ml_dtypes.bfloat16)


def density_pair(labels, jitter_0, jitter_1):
    heavy_a = jnp.where(labels == 1, jnp.float32(1.0), jnp.float32(0.2))
    heavy_b = jnp.where(labels == 1, jnp.float32(0.2), jnp.float32(1.0))
    return heavy_a * jitter_0, heavy_b * jitter_1


def populations_of(part, field, out_buf):
    _, levels, rows, lanes = field.shape
    width_x, width_y = rows - 8, lanes // 2
    depth = levels - 4
    lane = lax.broadcasted_iota(jnp.int32, (rows, width_y), 1)

    def moved(value, step, axis):
        return pltpu.roll(value, step % value.shape[axis], axis)

    def streamed(value, step_x, step_y):
        if step_y != 0:
            shift, edge = (1, 0) if step_y == 1 else (width_y - 1, width_y - 1)
            value = jnp.where(
                lane == edge,
                pltpu.roll(value[:, width_y:], shift, 1),
                pltpu.roll(value[:, :width_y], shift, 1),
            )
        if step_x != 0:
            value = moved(value, step_x, 0)
        return value[:width_x]

    other, around_x, around_y = [], [], []
    for level in range(levels):
        value = field[1 - part, level]
        other.append(value)
        around_x.append(moved(value, 1, 0) + moved(value, -1, 0))
        around_y.append(moved(value, 1, 1) + moved(value, -1, 1))
    flat_sum = [
        2.0 * other[level] + around_x[level] + around_y[level] for level in range(levels)
    ]
    gain = -1.6 / 36.0
    for level in range(1, levels - 1):
        between = 2.0 * other[level] + other[level + 1] + other[level - 1]
        tall_x = between + around_y[level]
        tall_y = between + around_x[level]
        speeds = (
            gain * (moved(tall_x, -1, 0) - moved(tall_x, 1, 0)),
            gain * (moved(tall_y, -1, 1) - moved(tall_y, 1, 1)),
            gain * (flat_sum[level + 1] - flat_sum[level - 1]),
        )
        density = field[part, level]
        squares = speeds[0] * speeds[0] + speeds[1] * speeds[1] + speeds[2] * speeds[2]
        rest = density * (1.0 - 1.875 * squares)
        scaled = {}
        for weight in sorted(set(WEIGHTS)):
            scaled[weight] = (
                weight * rest,
                (3.75 * weight) * density,
                (5.625 * weight) * density,
            )
        for number, (offsets, weight) in enumerate(zip(LATTICE, WEIGHTS)):
            target = level - 2 + offsets[2]
            if target < 0 or target >= depth:
                continue
            span = lanes if offsets[1] != 0 else width_y
            base, linear, square = (value[:, :span] for value in scaled[weight])
            along = None
            for step, speed in zip(offsets, speeds):
                if step != 0:
                    term = speed[:, :span]
                    if along is None:
                        along = term if step == 1 else -term
                    else:
                        along = along + term if step == 1 else along - term
            value = base
            if along is not None:
                value = base + along * (linear + square * along)
            out_buf[part * 19 + number, target] = streamed(value, offsets[0], offsets[1])


def exchange_kernel(
    sizes,
    labels_ref,
    jitter_ref,
    shells_ref,
    xtab_hbm,
    ytab_hbm,
    pop_ref,
    spec_ref,
    xtab,
    ytab,
    order_buf,
    plane_buf,
    half_send,
    half_buf,
    shell_own,
    shell_rows,
    shell_head,
    shell_pair,
    shell_next,
    shells_all,
    ymsg,
    ybuf,
    ext,
    xsend,
    xbuf,
    zsend,
    zbuf,
    zcol,
    zcol_buf,
    field,
    mask_h,
    mask_l,
    weighted,
    counts,
    power,
    row_send,
    row_buf,
    spec_send,
    spec_buf,
    tab_sem,
    p1_send,
    p1_recv,
    p2_send,
    p2_recv,
    s1_send,
    s1_recv,
    s2_send,
    s2_recv,
    y_send,
    y_recv,
    x_send,
    x_recv,
    z_send,
    z_recv,
    ar_send,
    ar_recv,
    as_send,
    as_recv,
):
    rows, secs, cols = sizes
    depth, width_x, width_y = labels_ref.shape
    full_x, full_y = width_x * rows, width_y * secs
    half = rows // 2
    row, sec, col = lax.axis_index("row"), lax.axis_index("sec"), lax.axis_index("col")
    hub = sec == 0

    def shifted(index, step, count):
        return lax.rem(index + step + count, count)

    barrier = pltpu.get_barrier_semaphore()
    for step in range(1, rows):
        pl.semaphore_signal(
            barrier, 1, device_id={"row": shifted(row, step, rows)}, device_id_type=MESH
        )
    for step in range(1, secs):
        pl.semaphore_signal(
            barrier, 1, device_id={"sec": shifted(sec, step, secs)}, device_id_type=MESH
        )
    for step in (1, -1):
        pl.semaphore_signal(
            barrier, 1, device_id={"col": shifted(col, step, cols)}, device_id_type=MESH
        )

    block = jnp.where(row < half, row, rows - 1 - row)
    xcopy = pltpu.make_async_copy(xtab_hbm.at[block], xtab, tab_sem.at[0])
    ycopy = pltpu.make_async_copy(ytab_hbm, ytab, tab_sem.at[1])
    xcopy.start()
    ycopy.start()

    rounded = []
    for plane in range(depth):
        pair = density_pair(labels_ref[plane], jitter_ref[0, plane], jitter_ref[1, plane])
        order_buf[plane] = (pair[0] - pair[1]).astype(jnp.bfloat16)
        rounded.append([value.astype(jnp.bfloat16) for value in pair])
    flat = jnp.concatenate(
        [rounded[plane][part] for part in range(2) for plane in range(depth)], axis=0
    )
    pick_row = lax.broadcasted_iota(jnp.int32, (8, width_y), 0)
    pick_lane = lax.broadcasted_iota(jnp.int32, (8, width_y), 1)
    near = (pick_row < 2) & (pick_lane == pick_row)
    far = (pick_row >= 6) & (pick_lane == pick_row + (width_y - 8))
    pick = jnp.where(near | far, 1.0, 0.0).astype(jnp.bfloat16)
    ymsg[...] = lax.dot_general(
        pick, flat, (((1,), (1,)), ((), ())), preferred_element_type=jnp.float32
    )
    shell_own[...] = shells_ref[...].astype(jnp.float32).astype(jnp.bfloat16)

    pl.semaphore_wait(barrier, rows + secs)

    waits = []

    def transfer(src, dst, ssem, rsem, target):
        return pltpu.make_async_remote_copy(
            src_ref=src,
            dst_ref=dst,
            send_sem=ssem,
            recv_sem=rsem,
            device_id=target,
            device_id_type=MESH,
        )

    def send(src, dst, ssem, rsem, target):
        copy = transfer(src, dst, ssem, rsem, target)
        copy.start()
        waits.append(copy)

    def arrive(dst, ssem, rsem, target):
        transfer(dst, dst, ssem, rsem, target).wait_recv()

    from_sec = jnp.maximum(sec - 1, 0)
    shell_copy = transfer(
        shell_own, shell_rows.at[sec], s2_send.at[0], s2_recv.at[from_sec], {"sec": 0}
    )

    @pl.when(sec > 0)
    def _():
        shell_copy.start()

    order = sorted(range(1, rows), key=lambda step: -min(step, rows - step))
    for step in order:
        target = shifted(row, step, rows)
        send(
            order_buf.at[target // half],
            plane_buf.at[row],
            p1_send.at[step - 1],
            p1_recv.at[step - 1],
            {"row": target},
        )
    for place, step in enumerate((1, -1)):
        send(
            ymsg,
            ybuf.at[place],
            y_send.at[place],
            y_recv.at[place],
            {"sec": shifted(sec, step, secs)},
        )
    plane_buf[row] = jnp.where(row < half, order_buf[0], order_buf[1])

    for place in range(2):
        arrive(ybuf.at[place], y_send.at[place], y_recv.at[place], {"sec": sec})
    lanes = flat.shape[0]
    side = lax.broadcasted_iota(jnp.int32, (8, lanes), 0) < 4
    columns = jnp.where(side, ybuf[1], ybuf[0])
    yhalo = lax.dot_general(
        columns.T.astype(jnp.bfloat16),
        pick,
        (((1,), (0,)), ((), ())),
        preferred_element_type=jnp.float32,
    )
    for part in range(2 * depth):
        begin = part * width_x
        ext[part, 0:width_x, 0:width_y] = flat[begin : begin + width_x].astype(jnp.float32)
        ext[part, 0:width_x, width_y : 2 * width_y] = yhalo[begin : begin + width_x]
    xsend[0] = ext[:, width_x - 8 : width_x, :]
    xsend[1] = ext[:, 0:8, :]
    for place, step in enumerate((1, -1)):
        send(
            xsend.at[place],
            xbuf.at[place],
            x_send.at[place],
            x_recv.at[place],
            {"row": shifted(row, step, rows)},
        )

    mirror = rows - 1 - row
    next_block = lax.rem(rows - row, half)
    pair_copy = transfer(
        shell_rows, shell_pair, s1_send.at[0], s1_recv.at[0], {"row": mirror}
    )
    next_copies = [
        transfer(
            shell_head,
            shell_next,
            s1_send.at[1 + place],
            s1_recv.at[1],
            {"row": target},
        )
        for place, target in enumerate((next_block, rows - 1 - next_block))
    ]

    @pl.when(hub)
    def _():
        shell_rows[0] = shell_own[...]
        for source in range(1, secs):
            arrive(shell_rows.at[source], s2_send.at[0], s2_recv.at[source - 1], {"sec": sec})
        shell_head[...] = shell_rows[:, 0:16, :]
        pair_copy.start()

        @pl.when(row >= half)
        def _():
            for copy in next_copies:
                copy.start()

    xcopy.wait()
    for step in order:
        arrive(
            plane_buf.at[shifted(row, -step, rows)],
            p1_send.at[step - 1],
            p1_recv.at[step - 1],
            {"row": row},
        )
    half_step = jnp.dot(
        xtab[...],
        plane_buf[...].reshape(full_x, width_y),
        preferred_element_type=jnp.float32,
    )
    half_send[...] = half_step.astype(jnp.bfloat16)
    half_copy = transfer(
        half_send, half_buf.at[sec], p2_send.at[0], p2_recv.at[from_sec], {"sec": 0}
    )

    @pl.when(sec > 0)
    def _():
        half_copy.start()

    for place in range(2):
        arrive(xbuf.at[place], x_send.at[place], x_recv.at[place], {"row": row})
    upper = lax.broadcasted_iota(jnp.int32, (2 * depth, 8, 2 * width_y), 1) < 4
    ext[:, width_x : width_x + 8, :] = jnp.where(upper, xbuf[1], xbuf[0])
    zsend[...] = ext[:, :, 0:width_y].reshape(zsend.shape).astype(jnp.bfloat16)
    margin = ext[:, :, width_y : 2 * width_y].reshape(zsend.shape).astype(jnp.bfloat16)
    blank = jnp.zeros((zcol.shape[1] - margin.shape[0], width_y), jnp.bfloat16)
    zcol[...] = lax.dot_general(
        pick,
        jnp.concatenate([margin, blank], axis=0),
        (((1,), (1,)), ((), ())),
        preferred_element_type=jnp.float32,
    )
    for place, step in enumerate((1, -1)):
        neighbour = {"col": shifted(col, step, cols)}
        send(zsend, zbuf.at[place], z_send.at[place], z_recv.at[place], neighbour)
        send(
            zcol, zcol_buf.at[place], z_send.at[2 + place], z_recv.at[2 + place], neighbour
        )
    shape = (2, depth, width_x + 8, 2 * width_y)
    field[:, depth : 2 * depth] = ext[...].reshape(shape)
    for plane in range(depth):
        pair = density_pair(labels_ref[plane], jitter_ref[0, plane], jitter_ref[1, plane])
        for part in range(2):
            field[part, depth + plane, 0:width_x, 0:width_y] = pair[part]

    lane = lax.broadcasted_iota(jnp.int32, (16, 128), 1)
    line_id = lax.broadcasted_iota(jnp.int32, (16, 256), 0)
    here = lax.broadcasted_iota(jnp.int32, (16, 256), 1) // 16 == line_id

    def spread(value):
        value = jnp.where(lane < 16, value, 0.0)
        for shift in (16, 32, 64):
            value = value + pltpu.roll(value, shift, 1)
        value = jnp.concatenate([value, value], axis=1)
        return jnp.sum(jnp.where(here, value, 0.0), axis=0, keepdims=True)

    def widen(value):
        blank = jnp.zeros((16, 128 - value.shape[1]), jnp.float32)
        return jnp.concatenate([value, blank], axis=1)

    def contract(left, right):
        return lax.dot_general(
            left, right, (((1,), (1,)), ((), ())), preferred_element_type=jnp.float32
        )

    @pl.when(hub)
    def _():
        arrive(shell_pair, s1_send.at[0], s1_recv.at[0], {"row": mirror})
        arrive(shell_next, s1_send.at[1], s1_recv.at[1], {"row": mirror})

        def joined(ref):
            return jnp.concatenate(
                [ref[source].astype(jnp.float32) for source in range(secs)], axis=1
            )

        mine, paired = joined(shell_rows), joined(shell_pair)
        minus = jnp.where(row < half, paired, mine)
        following = jnp.broadcast_to(joined(shell_next)[0:1], minus.shape)
        row_id = lax.broadcasted_iota(jnp.int32, minus.shape, 0)
        shells_all[0:width_x, :] = jnp.where(row < half, mine, paired)
        shells_all[width_x : 2 * width_x, :] = jnp.where(
            row_id == width_x - 1, following, pltpu.roll(minus, width_x - 1, 0)
        )
        tall = (16, full_y)
        label = lax.broadcasted_iota(jnp.int32, tall, 0).astype(jnp.float32)
        chunk = 8 * full_y

        def one_hot(digit):
            return jnp.where(jnp.broadcast_to(digit, tall) == label, 1.0, 0.0).astype(
                jnp.bfloat16
            )

        def build(step, total):
            value = shells_all[pl.ds(pl.multiple_of(step * 8, 8), 8), :]
            upper_digit = jnp.floor(value * (1.0 / 16.0))
            lower_digit = value - 16.0 * upper_digit
            begin = pl.multiple_of(step * chunk, chunk)
            for line in range(8):
                span = pl.ds(begin + line * full_y, full_y)
                mask_h[:, span] = one_hot(upper_digit[line : line + 1])
                mask_l[:, span] = one_hot(lower_digit[line : line + 1])
            span = pl.ds(begin, chunk)
            return total + contract(mask_h[:, span], mask_l[:, span])

        counts[...] = lax.fori_loop(
            0, 2 * width_x // 8, build, jnp.zeros((16, 16), jnp.float32)
        )

        ycopy.wait()
        half_buf[0] = half_send[...]
        for source in range(1, secs):
            arrive(
                half_buf.at[source], p2_send.at[0], p2_recv.at[source - 1], {"sec": sec}
            )
        left = jnp.concatenate([half_buf[source] for source in range(secs)], axis=1)
        product = jnp.dot(left, ytab[...], preferred_element_type=jnp.float32)
        re_cos, re_sin = product[:width_x, :full_y], product[:width_x, full_y:]
        im_cos, im_sin = product[width_x:, :full_y], product[width_x:, full_y:]
        first = (lax.broadcasted_iota(jnp.int32, (width_x, full_y), 0) == 0) & (block == 0)
        sum_re = jnp.where(first, re_cos, re_cos + im_sin)
        sum_im = jnp.where(first, re_sin, im_cos - re_sin)
        dif_re = jnp.where(first, im_cos, re_cos - im_sin)
        dif_im = jnp.where(first, im_sin, im_cos + re_sin)
        power[0] = sum_re * sum_re + sum_im * sum_im
        power[1] = dif_re * dif_re + dif_im * dif_im

        def gather(step, total):
            for sign in range(2):
                value = power[sign, pl.ds(pl.multiple_of(step * 8, 8), 8), :]
                coarse = value.astype(jnp.bfloat16).astype(jnp.float32)
                fine = value - coarse
                place = step if sign == 0 else 2 * width_x // 8 - 1 - step
                begin = pl.multiple_of(place * chunk, chunk)
                for line in range(8):
                    slot = line if sign == 0 else 7 - line
                    member = mask_l[:, pl.ds(begin + slot * full_y, full_y)]
                    span = slice(slot * full_y, (slot + 1) * full_y)
                    for half_id, part in enumerate((coarse, fine)):
                        line_value = jnp.broadcast_to(part[line : line + 1], tall)
                        weighted[sign, 16 * half_id : 16 * half_id + 16, span] = (
                            member * line_value.astype(jnp.bfloat16)
                        )
                total = total + contract(mask_h[:, pl.ds(begin, chunk)], weighted[sign])
            return total

        table = widen(
            lax.fori_loop(0, width_x // 8, gather, jnp.zeros((16, 32), jnp.float32))
        )
        row_send[0:1, :] = spread(table + pltpu.roll(table, 112, 1))
        row_send[1:2, :] = spread(widen(counts[...]))
        for step in order:
            transfer(
                row_send,
                row_buf.at[row],
                ar_send.at[step - 1],
                ar_recv.at[step - 1],
                {"row": shifted(row, step, rows)},
            ).start()
        row_buf[row] = row_send[...]

    for place, begin in enumerate((0, 2 * depth)):
        arrive(zbuf.at[place], z_send.at[place], z_recv.at[place], {"col": col})
        arrive(
            zcol_buf.at[place], z_send.at[2 + place], z_recv.at[2 + place], {"col": col}
        )
        side_shape = (2, depth, width_x + 8, width_y)
        margin = lax.dot_general(
            zcol_buf[place].T.astype(jnp.bfloat16),
            pick,
            (((1,), (0,)), ((), ())),
            preferred_element_type=jnp.float32,
        )[: zsend.shape[0]]
        field[:, begin : begin + depth, :, 0:width_y] = (
            zbuf[place].astype(jnp.float32).reshape(side_shape)
        )
        field[:, begin : begin + depth, :, width_y : 2 * width_y] = margin.reshape(side_shape)
    for part in range(2):
        populations_of(part, field, pop_ref)

    @pl.when(hub)
    def _():
        for step in order:
            arrive(
                row_buf.at[shifted(row, -step, rows)],
                ar_send.at[step - 1],
                ar_recv.at[step - 1],
                {"row": row},
            )
        sums = []
        for start in (0, half):
            total = row_buf[start]
            for source in range(start + 1, start + half):
                total = total + row_buf[source]
            sums.append(total)
        scale = sums[0][1:2] * float(full_x * full_y)
        spec_send[0:1, :] = sums[0][0:1] / scale
        spec_send[1:2, :] = sums[1][0:1] / scale
        spec_copies = [
            transfer(
                spec_send, spec_buf, as_send.at[target - 1], as_recv.at[0], {"sec": target}
            )
            for target in range(1, secs)
        ]
        for copy in spec_copies:
            copy.start()
        spec_ref[...] = spec_send[...]
        for copy in spec_copies:
            copy.wait_send()
        pair_copy.wait_send()

        @pl.when(row >= half)
        def _():
            for copy in next_copies:
                copy.wait_send()

        for step in order:
            transfer(
                row_send,
                row_buf.at[row],
                ar_send.at[step - 1],
                ar_recv.at[step - 1],
                {"row": row},
            ).wait_send()

    @pl.when(sec > 0)
    def _():
        arrive(spec_buf, as_send.at[0], as_recv.at[0], {"sec": sec})
        spec_ref[...] = spec_buf[...]
        ycopy.wait()
        shell_copy.wait_send()
        half_copy.wait_send()

    for copy in waits:
        copy.wait_send()


def exchange(labels, jitter, shells, sizes):
    rows, secs, _ = sizes
    depth, width_x, width_y = labels.shape
    full_x, full_y = width_x * rows, width_y * secs
    ext_rows = 2 * depth * (width_x + 8)
    col_lanes = -(-ext_rows // 128) * 128
    bf16, f32 = jnp.bfloat16, jnp.float32
    vmem = pl.BlockSpec(memory_space=pltpu.VMEM)
    hbm = pl.BlockSpec(memory_space=pl.ANY)
    dma = pltpu.SemaphoreType.DMA
    return pl.pallas_call(
        functools.partial(exchange_kernel, sizes),
        out_shape=(
            pltpu.VMEM((38, depth, width_x, width_y), f32),
            pltpu.VMEM((depth, NSHELL), f32),
        ),
        in_specs=[vmem, vmem, vmem, hbm, hbm],
        out_specs=(vmem, vmem),
        scratch_shapes=[
            pltpu.VMEM((2 * width_x, full_x), bf16),
            pltpu.VMEM((full_y, 2 * full_y), bf16),
            pltpu.VMEM((depth, width_x, width_y), bf16),
            pltpu.VMEM((rows, width_x, width_y), bf16),
            pltpu.VMEM((2 * width_x, width_y), bf16),
            pltpu.VMEM((secs, 2 * width_x, width_y), bf16),
            pltpu.VMEM((width_x, width_y), bf16),
            pltpu.VMEM((secs, width_x, width_y), bf16),
            pltpu.VMEM((secs, 16, width_y), bf16),
            pltpu.VMEM((secs, width_x, width_y), bf16),
            pltpu.VMEM((secs, 16, width_y), bf16),
            pltpu.VMEM((2 * width_x, full_y), f32),
            pltpu.VMEM((8, 2 * depth * width_x), f32),
            pltpu.VMEM((2, 8, 2 * depth * width_x), f32),
            pltpu.VMEM((2 * depth, width_x + 8, 2 * width_y), f32),
            pltpu.VMEM((2, 2 * depth, 8, 2 * width_y), f32),
            pltpu.VMEM((2, 2 * depth, 8, 2 * width_y), f32),
            pltpu.VMEM((ext_rows, width_y), bf16),
            pltpu.VMEM((2, ext_rows, width_y), bf16),
            pltpu.VMEM((8, col_lanes), f32),
            pltpu.VMEM((2, 8, col_lanes), f32),
            pltpu.VMEM((2, 3 * depth, width_x + 8, 2 * width_y), f32),
            pltpu.VMEM((16, 2 * width_x * full_y), bf16),
            pltpu.VMEM((16, 2 * width_x * full_y), bf16),
            pltpu.VMEM((2, 32, 8 * full_y), bf16),
            pltpu.VMEM((16, 16), f32),
            pltpu.VMEM((2, width_x, full_y), f32),
            pltpu.VMEM((2, NSHELL), f32),
            pltpu.VMEM((rows, 2, NSHELL), f32),
            pltpu.VMEM((2, NSHELL), f32),
            pltpu.VMEM((2, NSHELL), f32),
            dma((2,)),
            dma((rows - 1,)),
            dma((rows - 1,)),
            dma((1,)),
            dma((secs - 1,)),
            dma((3,)),
            dma((2,)),
            dma((1,)),
            dma((secs - 1,)),
            dma((2,)),
            dma((2,)),
            dma((2,)),
            dma((2,)),
            dma((4,)),
            dma((4,)),
            dma((rows - 1,)),
            dma((rows - 1,)),
            dma((secs - 1,)),
            dma((1,)),
        ],
        compiler_params=pltpu.CompilerParams(collective_id=0, has_side_effects=True),
        name="exchange",
    )(
        labels,
        jitter,
        shells,
        jnp.asarray(x_table(rows, width_x, full_x)),
        jnp.asarray(y_table(full_y)),
    )


def solution(mesh):
    sizes = tuple(mesh.shape[name] for name in ("row", "sec", "col"))

    def on_device(labels, jitter, shells):
        return exchange(labels, jitter, shells, sizes)

    in_specs = (P("col", "row", "sec"), P(None, "col", "row", "sec"), P("row", "sec"))
    out_specs = (P(None, "col", "row", "sec"), P("col", None))
    return jax.shard_map(
        on_device, mesh=mesh, in_specs=in_specs, out_specs=out_specs, check_vma=False
    )
```

```python
import functools
import math

import jax
import jax.numpy as jnp
import ml_dtypes
import numpy as np
from jax import lax
from jax.experimental import pallas as pl
from jax.experimental.pallas import tpu as pltpu
from jax.sharding import PartitionSpec as P

NSHELL = 256
MESH = pl.DeviceIdType.MESH

LATTICE = (
    (0, 0, 0),
    (1, 0, 0),
    (-1, 0, 0),
    (0, 1, 0),
    (0, -1, 0),
    (0, 0, 1),
    (0, 0, -1),
    (1, 1, 0),
    (-1, -1, 0),
    (1, -1, 0),
    (-1, 1, 0),
    (1, 0, 1),
    (-1, 0, -1),
    (1, 0, -1),
    (-1, 0, 1),
    (0, 1, 1),
    (0, -1, -1),
    (0, 1, -1),
    (0, -1, 1),
)
WEIGHTS = (1.0 / 3.0,) + (1.0 / 18.0,) * 6 + (1.0 / 36.0,) * 12


def trig(freq, pos, full):
    turn = (freq * pos % full).astype(np.float32) * np.float32(2.0 * math.pi / full)
    return np.cos(turn), np.sin(turn)


def x_table(rows, width, full):
    cos_x, sin_x = trig(np.arange(full // 2)[:, None], np.arange(full)[None, :], full)
    imag = -sin_x
    imag[0] = trig(full // 2, np.arange(full), full)[0]
    both = np.stack([cos_x, imag], 0).reshape(2, rows // 2, width, full)
    both = both.transpose(1, 0, 2, 3).reshape(rows // 2, 2 * width, full)
    return both.astype(ml_dtypes.bfloat16)


def y_table(full):
    cos_y, sin_y = trig(np.arange(full)[:, None], np.arange(full)[None, :], full)
    return np.concatenate([cos_y, sin_y], 1).astype(ml_dtypes.bfloat16)


def density_pair(labels, jitter_0, jitter_1):
    heavy_a = jnp.where(labels == 1, jnp.float32(1.0), jnp.float32(0.2))
    heavy_b = jnp.where(labels == 1, jnp.float32(0.2), jnp.float32(1.0))
    return heavy_a * jitter_0, heavy_b * jitter_1


def populations_of(part, field, out_buf):
    _, levels, rows, lanes = field.shape
    width_x, width_y = rows - 8, lanes // 2
    depth = levels - 4
    lane = lax.broadcasted_iota(jnp.int32, (rows, width_y), 1)

    def moved(value, step, axis):
        return pltpu.roll(value, step % value.shape[axis], axis)

    def streamed(value, step_x, step_y):
        if step_y != 0:
            shift, edge = (1, 0) if step_y == 1 else (width_y - 1, width_y - 1)
            value = jnp.where(
                lane == edge,
                pltpu.roll(value[:, width_y:], shift, 1),
                pltpu.roll(value[:, :width_y], shift, 1),
            )
        if step_x != 0:
            value = moved(value, step_x, 0)
        return value[:width_x]

    other, around_x, around_y = [], [], []
    for level in range(levels):
        value = field[1 - part, level]
        other.append(value)
        around_x.append(moved(value, 1, 0) + moved(value, -1, 0))
        around_y.append(moved(value, 1, 1) + moved(value, -1, 1))
    flat_sum = [
        2.0 * other[level] + around_x[level] + around_y[level] for level in range(levels)
    ]
    gain = -1.6 / 36.0
    for level in range(1, levels - 1):
        between = 2.0 * other[level] + other[level + 1] + other[level - 1]
        tall_x = between + around_y[level]
        tall_y = between + around_x[level]
        speeds = (
            gain * (moved(tall_x, -1, 0) - moved(tall_x, 1, 0)),
            gain * (moved(tall_y, -1, 1) - moved(tall_y, 1, 1)),
            gain * (flat_sum[level + 1] - flat_sum[level - 1]),
        )
        density = field[part, level]
        squares = speeds[0] * speeds[0] + speeds[1] * speeds[1] + speeds[2] * speeds[2]
        rest = density * (1.0 - 1.875 * squares)
        scaled = {}
        for weight in sorted(set(WEIGHTS)):
            scaled[weight] = (
                weight * rest,
                (3.75 * weight) * density,
                (5.625 * weight) * density,
            )
        for number, (offsets, weight) in enumerate(zip(LATTICE, WEIGHTS)):
            target = level - 2 + offsets[2]
            if target < 0 or target >= depth:
                continue
            span = lanes if offsets[1] != 0 else width_y
            base, linear, square = (value[:, :span] for value in scaled[weight])
            along = None
            for step, speed in zip(offsets, speeds):
                if step != 0:
                    term = speed[:, :span]
                    if along is None:
                        along = term if step == 1 else -term
                    else:
                        along = along + term if step == 1 else along - term
            value = base
            if along is not None:
                value = base + along * (linear + square * along)
            out_buf[part * 19 + number, target] = streamed(value, offsets[0], offsets[1])


def exchange_kernel(
    sizes,
    labels_ref,
    jitter_ref,
    shells_ref,
    xtab_hbm,
    ytab_hbm,
    pop_ref,
    spec_ref,
    xtab,
    ytab,
    order_buf,
    plane_buf,
    half_send,
    half_buf,
    shell_own,
    shell_rows,
    shell_head,
    shell_pair,
    shell_next,
    shells_all,
    ymsg,
    ybuf,
    ext,
    xsend,
    xbuf,
    zsend,
    zbuf,
    zcol,
    zcol_buf,
    field,
    mask_h,
    mask_l,
    weighted,
    counts,
    power,
    row_send,
    row_buf,
    spec_send,
    spec_buf,
    tab_sem,
    p1_send,
    p1_recv,
    p2_send,
    p2_recv,
    s1_send,
    s1_recv,
    s2_send,
    s2_recv,
    y_send,
    y_recv,
    x_send,
    x_recv,
    z_send,
    z_recv,
    ar_send,
    ar_recv,
    as_send,
    as_recv,
):
    rows, secs, cols = sizes
    depth, width_x, width_y = labels_ref.shape
    full_x, full_y = width_x * rows, width_y * secs
    half = rows // 2
    row, sec, col = lax.axis_index("row"), lax.axis_index("sec"), lax.axis_index("col")
    hub = sec == 0

    def shifted(index, step, count):
        return lax.rem(index + step + count, count)

    barrier = pltpu.get_barrier_semaphore()
    for step in range(1, rows):
        pl.semaphore_signal(
            barrier, 1, device_id={"row": shifted(row, step, rows)}, device_id_type=MESH
        )
    sec_steps = sorted({1, secs - 1})
    remote = (sec >= 2) & (sec <= secs - 2)
    for step in sec_steps:
        pl.semaphore_signal(
            barrier, 1, device_id={"sec": shifted(sec, step, secs)}, device_id_type=MESH
        )

    @pl.when(hub)
    def _():
        for target in range(2, secs - 1):
            pl.semaphore_signal(
                barrier, 1, device_id={"sec": target}, device_id_type=MESH
            )

    @pl.when(remote)
    def _():
        pl.semaphore_signal(barrier, 1, device_id={"sec": 0}, device_id_type=MESH)

    for step in (1, -1):
        pl.semaphore_signal(
            barrier, 1, device_id={"col": shifted(col, step, cols)}, device_id_type=MESH
        )

    block = jnp.where(row < half, row, rows - 1 - row)
    xcopy = pltpu.make_async_copy(xtab_hbm.at[block], xtab, tab_sem.at[0])
    ycopy = pltpu.make_async_copy(ytab_hbm, ytab, tab_sem.at[1])
    xcopy.start()
    ycopy.start()

    rounded = []
    for plane in range(depth):
        pair = density_pair(labels_ref[plane], jitter_ref[0, plane], jitter_ref[1, plane])
        order_buf[plane] = (pair[0] - pair[1]).astype(jnp.bfloat16)
        rounded.append([value.astype(jnp.bfloat16) for value in pair])
    flat = jnp.concatenate(
        [rounded[plane][part] for part in range(2) for plane in range(depth)], axis=0
    )
    pick_row = lax.broadcasted_iota(jnp.int32, (8, width_y), 0)
    pick_lane = lax.broadcasted_iota(jnp.int32, (8, width_y), 1)
    near = (pick_row < 2) & (pick_lane == pick_row)
    far = (pick_row >= 6) & (pick_lane == pick_row + (width_y - 8))
    pick = jnp.where(near | far, 1.0, 0.0).astype(jnp.bfloat16)
    ymsg[...] = lax.dot_general(
        pick, flat, (((1,), (1,)), ((), ())), preferred_element_type=jnp.float32
    )
    shell_own[...] = shells_ref[...].astype(jnp.float32).astype(jnp.bfloat16)

    greeters = rows - 1 + len(sec_steps) + 2
    extra = jnp.where(hub, max(secs - 3, 0), jnp.where(remote, 1, 0))
    pl.semaphore_wait(barrier, greeters + extra)

    waits = []

    def transfer(src, dst, ssem, rsem, target):
        return pltpu.make_async_remote_copy(
            src_ref=src,
            dst_ref=dst,
            send_sem=ssem,
            recv_sem=rsem,
            device_id=target,
            device_id_type=MESH,
        )

    def send(src, dst, ssem, rsem, target):
        copy = transfer(src, dst, ssem, rsem, target)
        copy.start()
        waits.append(copy)

    def arrive(dst, ssem, rsem, target):
        transfer(dst, dst, ssem, rsem, target).wait_recv()

    from_sec = jnp.maximum(sec - 1, 0)
    shell_copy = transfer(
        shell_own, shell_rows.at[sec], s2_send.at[0], s2_recv.at[from_sec], {"sec": 0}
    )

    @pl.when(sec > 0)
    def _():
        shell_copy.start()

    order = sorted(range(1, rows), key=lambda step: -min(step, rows - step))
    for step in order:
        target = shifted(row, step, rows)
        send(
            order_buf.at[target // half],
            plane_buf.at[row],
            p1_send.at[step - 1],
            p1_recv.at[step - 1],
            {"row": target},
        )
    for place, step in enumerate((1, -1)):
        send(
            ymsg,
            ybuf.at[place],
            y_send.at[place],
            y_recv.at[place],
            {"sec": shifted(sec, step, secs)},
        )
    plane_buf[row] = jnp.where(row < half, order_buf[0], order_buf[1])

    xcopy.wait()
    for step in order:
        arrive(
            plane_buf.at[shifted(row, -step, rows)],
            p1_send.at[step - 1],
            p1_recv.at[step - 1],
            {"row": row},
        )
    half_step = jnp.dot(
        xtab[...],
        plane_buf[...].reshape(full_x, width_y),
        preferred_element_type=jnp.float32,
    )
    half_send[...] = half_step.astype(jnp.bfloat16)
    half_copy = transfer(
        half_send, half_buf.at[sec], p2_send.at[0], p2_recv.at[from_sec], {"sec": 0}
    )

    @pl.when(sec > 0)
    def _():
        half_copy.start()

    for place in range(2):
        arrive(ybuf.at[place], y_send.at[place], y_recv.at[place], {"sec": sec})
    lanes = flat.shape[0]
    side = lax.broadcasted_iota(jnp.int32, (8, lanes), 0) < 4
    columns = jnp.where(side, ybuf[1], ybuf[0])
    yhalo = lax.dot_general(
        columns.T.astype(jnp.bfloat16),
        pick,
        (((1,), (0,)), ((), ())),
        preferred_element_type=jnp.float32,
    )
    for part in range(2 * depth):
        begin = part * width_x
        ext[part, 0:width_x, 0:width_y] = flat[begin : begin + width_x].astype(jnp.float32)
        ext[part, 0:width_x, width_y : 2 * width_y] = yhalo[begin : begin + width_x]
    xsend[0] = ext[:, width_x - 8 : width_x, :]
    xsend[1] = ext[:, 0:8, :]
    for place, step in enumerate((1, -1)):
        send(
            xsend.at[place],
            xbuf.at[place],
            x_send.at[place],
            x_recv.at[place],
            {"row": shifted(row, step, rows)},
        )

    mirror = rows - 1 - row
    next_block = lax.rem(rows - row, half)
    pair_copy = transfer(
        shell_rows, shell_pair, s1_send.at[0], s1_recv.at[0], {"row": mirror}
    )
    next_copies = [
        transfer(
            shell_head,
            shell_next,
            s1_send.at[1 + place],
            s1_recv.at[1],
            {"row": target},
        )
        for place, target in enumerate((next_block, rows - 1 - next_block))
    ]

    @pl.when(hub)
    def _():
        shell_rows[0] = shell_own[...]
        for source in range(1, secs):
            arrive(shell_rows.at[source], s2_send.at[0], s2_recv.at[source - 1], {"sec": sec})
        shell_head[...] = shell_rows[:, 0:16, :]
        pair_copy.start()

        @pl.when(row >= half)
        def _():
            for copy in next_copies:
                copy.start()

    for place in range(2):
        arrive(xbuf.at[place], x_send.at[place], x_recv.at[place], {"row": row})
    upper = lax.broadcasted_iota(jnp.int32, (2 * depth, 8, 2 * width_y), 1) < 4
    ext[:, width_x : width_x + 8, :] = jnp.where(upper, xbuf[1], xbuf[0])
    zsend[...] = ext[:, :, 0:width_y].reshape(zsend.shape).astype(jnp.bfloat16)
    margin = ext[:, :, width_y : 2 * width_y].reshape(zsend.shape).astype(jnp.bfloat16)
    blank = jnp.zeros((zcol.shape[1] - margin.shape[0], width_y), jnp.bfloat16)
    zcol[...] = lax.dot_general(
        pick,
        jnp.concatenate([margin, blank], axis=0),
        (((1,), (1,)), ((), ())),
        preferred_element_type=jnp.float32,
    )
    for place, step in enumerate((1, -1)):
        neighbour = {"col": shifted(col, step, cols)}
        send(zsend, zbuf.at[place], z_send.at[place], z_recv.at[place], neighbour)
        send(
            zcol, zcol_buf.at[place], z_send.at[2 + place], z_recv.at[2 + place], neighbour
        )
    shape = (2, depth, width_x + 8, 2 * width_y)
    field[:, depth : 2 * depth] = ext[...].reshape(shape)
    for plane in range(depth):
        pair = density_pair(labels_ref[plane], jitter_ref[0, plane], jitter_ref[1, plane])
        for part in range(2):
            field[part, depth + plane, 0:width_x, 0:width_y] = pair[part]

    lane = lax.broadcasted_iota(jnp.int32, (16, 128), 1)
    line_id = lax.broadcasted_iota(jnp.int32, (16, 256), 0)
    here = lax.broadcasted_iota(jnp.int32, (16, 256), 1) // 16 == line_id

    def spread(value):
        value = jnp.where(lane < 16, value, 0.0)
        for shift in (16, 32, 64):
            value = value + pltpu.roll(value, shift, 1)
        value = jnp.concatenate([value, value], axis=1)
        return jnp.sum(jnp.where(here, value, 0.0), axis=0, keepdims=True)

    def widen(value):
        blank = jnp.zeros((16, 128 - value.shape[1]), jnp.float32)
        return jnp.concatenate([value, blank], axis=1)

    def contract(left, right):
        return lax.dot_general(
            left, right, (((1,), (1,)), ((), ())), preferred_element_type=jnp.float32
        )

    @pl.when(hub)
    def _():
        arrive(shell_pair, s1_send.at[0], s1_recv.at[0], {"row": mirror})
        arrive(shell_next, s1_send.at[1], s1_recv.at[1], {"row": mirror})

        def joined(ref):
            return jnp.concatenate(
                [ref[source].astype(jnp.float32) for source in range(secs)], axis=1
            )

        mine, paired = joined(shell_rows), joined(shell_pair)
        minus = jnp.where(row < half, paired, mine)
        following = jnp.broadcast_to(joined(shell_next)[0:1], minus.shape)
        row_id = lax.broadcasted_iota(jnp.int32, minus.shape, 0)
        shells_all[0:width_x, :] = jnp.where(row < half, mine, paired)
        shells_all[width_x : 2 * width_x, :] = jnp.where(
            row_id == width_x - 1, following, pltpu.roll(minus, width_x - 1, 0)
        )
        tall = (16, full_y)
        label = lax.broadcasted_iota(jnp.int32, tall, 0).astype(jnp.float32)
        chunk = 8 * full_y

        def one_hot(digit):
            return jnp.where(jnp.broadcast_to(digit, tall) == label, 1.0, 0.0).astype(
                jnp.bfloat16
            )

        def build(step, total):
            value = shells_all[pl.ds(pl.multiple_of(step * 8, 8), 8), :]
            upper_digit = jnp.floor(value * (1.0 / 16.0))
            lower_digit = value - 16.0 * upper_digit
            begin = pl.multiple_of(step * chunk, chunk)
            for line in range(8):
                span = pl.ds(begin + line * full_y, full_y)
                mask_h[:, span] = one_hot(upper_digit[line : line + 1])
                mask_l[:, span] = one_hot(lower_digit[line : line + 1])
            span = pl.ds(begin, chunk)
            return total + contract(mask_h[:, span], mask_l[:, span])

        counts[...] = lax.fori_loop(
            0, 2 * width_x // 8, build, jnp.zeros((16, 16), jnp.float32)
        )

        ycopy.wait()
        half_buf[0] = half_send[...]
        for source in range(1, secs):
            arrive(
                half_buf.at[source], p2_send.at[0], p2_recv.at[source - 1], {"sec": sec}
            )
        left = jnp.concatenate([half_buf[source] for source in range(secs)], axis=1)
        product = jnp.dot(left, ytab[...], preferred_element_type=jnp.float32)
        re_cos, re_sin = product[:width_x, :full_y], product[:width_x, full_y:]
        im_cos, im_sin = product[width_x:, :full_y], product[width_x:, full_y:]
        first = (lax.broadcasted_iota(jnp.int32, (width_x, full_y), 0) == 0) & (block == 0)
        sum_re = jnp.where(first, re_cos, re_cos + im_sin)
        sum_im = jnp.where(first, re_sin, im_cos - re_sin)
        dif_re = jnp.where(first, im_cos, re_cos - im_sin)
        dif_im = jnp.where(first, im_sin, im_cos + re_sin)
        power[0] = sum_re * sum_re + sum_im * sum_im
        power[1] = dif_re * dif_re + dif_im * dif_im

        def gather(step, total):
            for sign in range(2):
                value = power[sign, pl.ds(pl.multiple_of(step * 8, 8), 8), :]
                coarse = value.astype(jnp.bfloat16).astype(jnp.float32)
                fine = value - coarse
                place = step if sign == 0 else 2 * width_x // 8 - 1 - step
                begin = pl.multiple_of(place * chunk, chunk)
                for line in range(8):
                    slot = line if sign == 0 else 7 - line
                    member = mask_l[:, pl.ds(begin + slot * full_y, full_y)]
                    span = slice(slot * full_y, (slot + 1) * full_y)
                    for half_id, part in enumerate((coarse, fine)):
                        line_value = jnp.broadcast_to(part[line : line + 1], tall)
                        weighted[sign, 16 * half_id : 16 * half_id + 16, span] = (
                            member * line_value.astype(jnp.bfloat16)
                        )
                total = total + contract(mask_h[:, pl.ds(begin, chunk)], weighted[sign])
            return total

        table = widen(
            lax.fori_loop(0, width_x // 8, gather, jnp.zeros((16, 32), jnp.float32))
        )
        row_send[0:1, :] = spread(table + pltpu.roll(table, 112, 1))
        row_send[1:2, :] = spread(widen(counts[...]))
        for step in order:
            transfer(
                row_send,
                row_buf.at[row],
                ar_send.at[step - 1],
                ar_recv.at[step - 1],
                {"row": shifted(row, step, rows)},
            ).start()
        row_buf[row] = row_send[...]

    for place, begin in enumerate((0, 2 * depth)):
        arrive(zbuf.at[place], z_send.at[place], z_recv.at[place], {"col": col})
        arrive(
            zcol_buf.at[place], z_send.at[2 + place], z_recv.at[2 + place], {"col": col}
        )
        side_shape = (2, depth, width_x + 8, width_y)
        margin = lax.dot_general(
            zcol_buf[place].T.astype(jnp.bfloat16),
            pick,
            (((1,), (0,)), ((), ())),
            preferred_element_type=jnp.float32,
        )[: zsend.shape[0]]
        field[:, begin : begin + depth, :, 0:width_y] = (
            zbuf[place].astype(jnp.float32).reshape(side_shape)
        )
        field[:, begin : begin + depth, :, width_y : 2 * width_y] = margin.reshape(side_shape)
    for part in range(2):
        populations_of(part, field, pop_ref)

    @pl.when(hub)
    def _():
        for step in order:
            arrive(
                row_buf.at[shifted(row, -step, rows)],
                ar_send.at[step - 1],
                ar_recv.at[step - 1],
                {"row": row},
            )
        sums = []
        for start in (0, half):
            total = row_buf[start]
            for source in range(start + 1, start + half):
                total = total + row_buf[source]
            sums.append(total)
        scale = sums[0][1:2] * float(full_x * full_y)
        spec_send[0:1, :] = sums[0][0:1] / scale
        spec_send[1:2, :] = sums[1][0:1] / scale
        spec_copies = [
            transfer(
                spec_send, spec_buf, as_send.at[target - 1], as_recv.at[0], {"sec": target}
            )
            for target in range(1, secs)
        ]
        for copy in spec_copies:
            copy.start()
        spec_ref[...] = spec_send[...]
        for copy in spec_copies:
            copy.wait_send()
        pair_copy.wait_send()

        @pl.when(row >= half)
        def _():
            for copy in next_copies:
                copy.wait_send()

        for step in order:
            transfer(
                row_send,
                row_buf.at[row],
                ar_send.at[step - 1],
                ar_recv.at[step - 1],
                {"row": row},
            ).wait_send()

    @pl.when(sec > 0)
    def _():
        arrive(spec_buf, as_send.at[0], as_recv.at[0], {"sec": sec})
        spec_ref[...] = spec_buf[...]
        ycopy.wait()
        shell_copy.wait_send()
        half_copy.wait_send()

    for copy in waits:
        copy.wait_send()


def exchange(labels, jitter, shells, sizes):
    rows, secs, _ = sizes
    depth, width_x, width_y = labels.shape
    full_x, full_y = width_x * rows, width_y * secs
    ext_rows = 2 * depth * (width_x + 8)
    col_lanes = -(-ext_rows // 128) * 128
    bf16, f32 = jnp.bfloat16, jnp.float32
    vmem = pl.BlockSpec(memory_space=pltpu.VMEM)
    hbm = pl.BlockSpec(memory_space=pl.ANY)
    dma = pltpu.SemaphoreType.DMA
    return pl.pallas_call(
        functools.partial(exchange_kernel, sizes),
        out_shape=(
            pltpu.VMEM((38, depth, width_x, width_y), f32),
            pltpu.VMEM((depth, NSHELL), f32),
        ),
        in_specs=[vmem, vmem, vmem, hbm, hbm],
        out_specs=(vmem, vmem),
        scratch_shapes=[
            pltpu.VMEM((2 * width_x, full_x), bf16),
            pltpu.VMEM((full_y, 2 * full_y), bf16),
            pltpu.VMEM((depth, width_x, width_y), bf16),
            pltpu.VMEM((rows, width_x, width_y), bf16),
            pltpu.VMEM((2 * width_x, width_y), bf16),
            pltpu.VMEM((secs, 2 * width_x, width_y), bf16),
            pltpu.VMEM((width_x, width_y), bf16),
            pltpu.VMEM((secs, width_x, width_y), bf16),
            pltpu.VMEM((secs, 16, width_y), bf16),
            pltpu.VMEM((secs, width_x, width_y), bf16),
            pltpu.VMEM((secs, 16, width_y), bf16),
            pltpu.VMEM((2 * width_x, full_y), f32),
            pltpu.VMEM((8, 2 * depth * width_x), f32),
            pltpu.VMEM((2, 8, 2 * depth * width_x), f32),
            pltpu.VMEM((2 * depth, width_x + 8, 2 * width_y), f32),
            pltpu.VMEM((2, 2 * depth, 8, 2 * width_y), f32),
            pltpu.VMEM((2, 2 * depth, 8, 2 * width_y), f32),
            pltpu.VMEM((ext_rows, width_y), bf16),
            pltpu.VMEM((2, ext_rows, width_y), bf16),
            pltpu.VMEM((8, col_lanes), f32),
            pltpu.VMEM((2, 8, col_lanes), f32),
            pltpu.VMEM((2, 3 * depth, width_x + 8, 2 * width_y), f32),
            pltpu.VMEM((16, 2 * width_x * full_y), bf16),
            pltpu.VMEM((16, 2 * width_x * full_y), bf16),
            pltpu.VMEM((2, 32, 8 * full_y), bf16),
            pltpu.VMEM((16, 16), f32),
            pltpu.VMEM((2, width_x, full_y), f32),
            pltpu.VMEM((2, NSHELL), f32),
            pltpu.VMEM((rows, 2, NSHELL), f32),
            pltpu.VMEM((2, NSHELL), f32),
            pltpu.VMEM((2, NSHELL), f32),
            dma((2,)),
            dma((rows - 1,)),
            dma((rows - 1,)),
            dma((1,)),
            dma((secs - 1,)),
            dma((3,)),
            dma((2,)),
            dma((1,)),
            dma((secs - 1,)),
            dma((2,)),
            dma((2,)),
            dma((2,)),
            dma((2,)),
            dma((4,)),
            dma((4,)),
            dma((rows - 1,)),
            dma((rows - 1,)),
            dma((secs - 1,)),
            dma((1,)),
        ],
        compiler_params=pltpu.CompilerParams(collective_id=0, has_side_effects=True),
        name="exchange",
    )(
        labels,
        jitter,
        shells,
        jnp.asarray(x_table(rows, width_x, full_x)),
        jnp.asarray(y_table(full_y)),
    )


def solution(mesh):
    sizes = tuple(mesh.shape[name] for name in ("row", "sec", "col"))

    def on_device(labels, jitter, shells):
        return exchange(labels, jitter, shells, sizes)

    in_specs = (P("col", "row", "sec"), P(None, "col", "row", "sec"), P("row", "sec"))
    out_specs = (P(None, "col", "row", "sec"), P("col", None))
    return jax.shard_map(
        on_device, mesh=mesh, in_specs=in_specs, out_specs=out_specs, check_vma=False
    )
```

```python
import functools
import math

import jax
import jax.numpy as jnp
import ml_dtypes
import numpy as np
from jax import lax
from jax.experimental import pallas as pl
from jax.experimental.pallas import tpu as pltpu
from jax.sharding import PartitionSpec as P

NSHELL = 256
MESH = pl.DeviceIdType.MESH

LATTICE = (
    (0, 0, 0),
    (1, 0, 0),
    (-1, 0, 0),
    (0, 1, 0),
    (0, -1, 0),
    (0, 0, 1),
    (0, 0, -1),
    (1, 1, 0),
    (-1, -1, 0),
    (1, -1, 0),
    (-1, 1, 0),
    (1, 0, 1),
    (-1, 0, -1),
    (1, 0, -1),
    (-1, 0, 1),
    (0, 1, 1),
    (0, -1, -1),
    (0, 1, -1),
    (0, -1, 1),
)
WEIGHTS = (1.0 / 3.0,) + (1.0 / 18.0,) * 6 + (1.0 / 36.0,) * 12


def trig(freq, pos, full):
    turn = (freq * pos % full).astype(np.float32) * np.float32(2.0 * math.pi / full)
    return np.cos(turn), np.sin(turn)


def x_table(rows, width, full):
    cos_x, sin_x = trig(np.arange(full // 2)[:, None], np.arange(full)[None, :], full)
    imag = -sin_x
    imag[0] = trig(full // 2, np.arange(full), full)[0]
    both = np.stack([cos_x, imag], 0).reshape(2, rows // 2, width, full)
    both = both.transpose(1, 0, 2, 3).reshape(rows // 2, 2 * width, full)
    return both.astype(ml_dtypes.bfloat16)


def y_table(full):
    cos_y, sin_y = trig(np.arange(full)[:, None], np.arange(full)[None, :], full)
    return np.concatenate([cos_y, sin_y], 1).astype(ml_dtypes.bfloat16)


def density_pair(labels, jitter_0, jitter_1):
    heavy_a = jnp.where(labels == 1, jnp.float32(1.0), jnp.float32(0.2))
    heavy_b = jnp.where(labels == 1, jnp.float32(0.2), jnp.float32(1.0))
    return heavy_a * jitter_0, heavy_b * jitter_1


def populations_of(part, field, out_buf):
    _, levels, rows, lanes = field.shape
    width_x, width_y = rows - 8, lanes // 2
    depth = levels - 4
    lane = lax.broadcasted_iota(jnp.int32, (rows, width_y), 1)

    def moved(value, step, axis):
        return pltpu.roll(value, step % value.shape[axis], axis)

    def streamed(value, step_x, step_y):
        if step_y != 0:
            shift, edge = (1, 0) if step_y == 1 else (width_y - 1, width_y - 1)
            value = jnp.where(
                lane == edge,
                pltpu.roll(value[:, width_y:], shift, 1),
                pltpu.roll(value[:, :width_y], shift, 1),
            )
        if step_x != 0:
            value = moved(value, step_x, 0)
        return value[:width_x]

    other, around_x, around_y = [], [], []
    for level in range(levels):
        value = field[1 - part, level]
        other.append(value)
        around_x.append(moved(value, 1, 0) + moved(value, -1, 0))
        around_y.append(moved(value, 1, 1) + moved(value, -1, 1))
    flat_sum = [
        2.0 * other[level] + around_x[level] + around_y[level] for level in range(levels)
    ]
    gain = -1.6 / 36.0
    for level in range(1, levels - 1):
        between = 2.0 * other[level] + other[level + 1] + other[level - 1]
        tall_x = between + around_y[level]
        tall_y = between + around_x[level]
        speeds = (
            gain * (moved(tall_x, -1, 0) - moved(tall_x, 1, 0)),
            gain * (moved(tall_y, -1, 1) - moved(tall_y, 1, 1)),
            gain * (flat_sum[level + 1] - flat_sum[level - 1]),
        )
        density = field[part, level]
        squares = speeds[0] * speeds[0] + speeds[1] * speeds[1] + speeds[2] * speeds[2]
        rest = density * (1.0 - 1.875 * squares)
        scaled = {}
        for weight in sorted(set(WEIGHTS)):
            scaled[weight] = (
                weight * rest,
                (3.75 * weight) * density,
                (5.625 * weight) * density,
            )
        for number, (offsets, weight) in enumerate(zip(LATTICE, WEIGHTS)):
            target = level - 2 + offsets[2]
            if target < 0 or target >= depth:
                continue
            span = lanes if offsets[1] != 0 else width_y
            base, linear, square = (value[:, :span] for value in scaled[weight])
            along = None
            for step, speed in zip(offsets, speeds):
                if step != 0:
                    term = speed[:, :span]
                    if along is None:
                        along = term if step == 1 else -term
                    else:
                        along = along + term if step == 1 else along - term
            value = base
            if along is not None:
                value = base + along * (linear + square * along)
            out_buf[part * 19 + number, target] = streamed(value, offsets[0], offsets[1])


def exchange_kernel(
    sizes,
    labels_ref,
    jitter_ref,
    shells_ref,
    xtab_hbm,
    ytab_hbm,
    pop_ref,
    spec_ref,
    xtab,
    ytab,
    order_buf,
    plane_buf,
    half_send,
    half_buf,
    shell_own,
    shell_rows,
    shell_head,
    shell_pair,
    shell_next,
    shells_all,
    ymsg,
    ybuf,
    ext,
    xsend,
    xbuf,
    zsend,
    zbuf,
    zcol,
    zcol_buf,
    field,
    mask_h,
    mask_l,
    weighted,
    counts,
    power,
    row_send,
    row_buf,
    spec_send,
    spec_buf,
    tab_sem,
    p1_send,
    p1_recv,
    p2_send,
    p2_recv,
    s1_send,
    s1_recv,
    s2_send,
    s2_recv,
    y_send,
    y_recv,
    x_send,
    x_recv,
    z_send,
    z_recv,
    ar_send,
    ar_recv,
    as_send,
    as_recv,
):
    rows, secs, cols = sizes
    depth, width_x, width_y = labels_ref.shape
    full_x, full_y = width_x * rows, width_y * secs
    half = rows // 2
    row, sec, col = lax.axis_index("row"), lax.axis_index("sec"), lax.axis_index("col")
    hub = sec == 0

    def shifted(index, step, count):
        return lax.rem(index + step + count, count)

    barrier = pltpu.get_barrier_semaphore()
    for step in range(1, rows):
        pl.semaphore_signal(
            barrier, 1, device_id={"row": shifted(row, step, rows)}, device_id_type=MESH
        )
    sec_steps = sorted({1, secs - 1})
    remote = (sec >= 2) & (sec <= secs - 2)
    for step in sec_steps:
        pl.semaphore_signal(
            barrier, 1, device_id={"sec": shifted(sec, step, secs)}, device_id_type=MESH
        )

    @pl.when(hub)
    def _():
        for target in range(2, secs - 1):
            pl.semaphore_signal(
                barrier, 1, device_id={"sec": target}, device_id_type=MESH
            )

    @pl.when(remote)
    def _():
        pl.semaphore_signal(barrier, 1, device_id={"sec": 0}, device_id_type=MESH)

    for step in (1, -1):
        pl.semaphore_signal(
            barrier, 1, device_id={"col": shifted(col, step, cols)}, device_id_type=MESH
        )

    block = jnp.where(row < half, row, rows - 1 - row)
    xcopy = pltpu.make_async_copy(xtab_hbm.at[block], xtab, tab_sem.at[0])
    ycopy = pltpu.make_async_copy(ytab_hbm, ytab, tab_sem.at[1])
    xcopy.start()
    ycopy.start()

    rounded = []
    for plane in range(depth):
        pair = density_pair(labels_ref[plane], jitter_ref[0, plane], jitter_ref[1, plane])
        order_buf[plane] = (pair[0] - pair[1]).astype(jnp.bfloat16)
        rounded.append([value.astype(jnp.bfloat16) for value in pair])
    flat = jnp.concatenate(
        [rounded[plane][part] for part in range(2) for plane in range(depth)], axis=0
    )
    pick_row = lax.broadcasted_iota(jnp.int32, (8, width_y), 0)
    pick_lane = lax.broadcasted_iota(jnp.int32, (8, width_y), 1)
    near = (pick_row < 2) & (pick_lane == pick_row)
    far = (pick_row >= 6) & (pick_lane == pick_row + (width_y - 8))
    pick = jnp.where(near | far, 1.0, 0.0).astype(jnp.bfloat16)
    ymsg[...] = lax.dot_general(
        pick, flat, (((1,), (1,)), ((), ())), preferred_element_type=jnp.float32
    )
    shell_own[...] = shells_ref[...].astype(jnp.float32).astype(jnp.bfloat16)

    greeters = rows - 1 + len(sec_steps) + 2
    extra = jnp.where(hub, max(secs - 3, 0), jnp.where(remote, 1, 0))
    pl.semaphore_wait(barrier, greeters + extra)

    waits = []

    def transfer(src, dst, ssem, rsem, target):
        return pltpu.make_async_remote_copy(
            src_ref=src,
            dst_ref=dst,
            send_sem=ssem,
            recv_sem=rsem,
            device_id=target,
            device_id_type=MESH,
        )

    def send(src, dst, ssem, rsem, target):
        copy = transfer(src, dst, ssem, rsem, target)
        copy.start()
        waits.append(copy)

    def arrive(dst, ssem, rsem, target):
        transfer(dst, dst, ssem, rsem, target).wait_recv()

    from_sec = jnp.maximum(sec - 1, 0)
    shell_copy = transfer(
        shell_own, shell_rows.at[sec], s2_send.at[0], s2_recv.at[from_sec], {"sec": 0}
    )

    @pl.when(sec > 0)
    def _():
        shell_copy.start()

    order = sorted(range(1, rows), key=lambda step: -min(step, rows - step))
    for step in order:
        target = shifted(row, step, rows)
        send(
            order_buf.at[target // half],
            plane_buf.at[row],
            p1_send.at[step - 1],
            p1_recv.at[step - 1],
            {"row": target},
        )
    for place, step in enumerate((1, -1)):
        send(
            ymsg,
            ybuf.at[place],
            y_send.at[place],
            y_recv.at[place],
            {"sec": shifted(sec, step, secs)},
        )
    plane_buf[row] = jnp.where(row < half, order_buf[0], order_buf[1])

    xcopy.wait()
    for step in order:
        arrive(
            plane_buf.at[shifted(row, -step, rows)],
            p1_send.at[step - 1],
            p1_recv.at[step - 1],
            {"row": row},
        )
    half_step = jnp.dot(
        xtab[...],
        plane_buf[...].reshape(full_x, width_y),
        preferred_element_type=jnp.float32,
    )
    half_send[...] = half_step.astype(jnp.bfloat16)
    half_copy = transfer(
        half_send, half_buf.at[sec], p2_send.at[0], p2_recv.at[from_sec], {"sec": 0}
    )

    @pl.when(sec > 0)
    def _():
        half_copy.start()

    mirror = rows - 1 - row
    next_block = lax.rem(rows - row, half)
    pair_copy = transfer(
        shell_rows, shell_pair, s1_send.at[0], s1_recv.at[0], {"row": mirror}
    )
    next_copies = [
        transfer(
            shell_head,
            shell_next,
            s1_send.at[1 + place],
            s1_recv.at[1],
            {"row": target},
        )
        for place, target in enumerate((next_block, rows - 1 - next_block))
    ]

    @pl.when(hub)
    def _():
        shell_rows[0] = shell_own[...]
        for source in range(1, secs):
            arrive(shell_rows.at[source], s2_send.at[0], s2_recv.at[source - 1], {"sec": sec})
        shell_head[...] = shell_rows[:, 0:16, :]
        pair_copy.start()

        @pl.when(row >= half)
        def _():
            for copy in next_copies:
                copy.start()

    for place in range(2):
        arrive(ybuf.at[place], y_send.at[place], y_recv.at[place], {"sec": sec})
    lanes = flat.shape[0]
    side = lax.broadcasted_iota(jnp.int32, (8, lanes), 0) < 4
    columns = jnp.where(side, ybuf[1], ybuf[0])
    yhalo = lax.dot_general(
        columns.T.astype(jnp.bfloat16),
        pick,
        (((1,), (0,)), ((), ())),
        preferred_element_type=jnp.float32,
    )
    for part in range(2 * depth):
        begin = part * width_x
        ext[part, 0:width_x, 0:width_y] = flat[begin : begin + width_x].astype(jnp.float32)
        ext[part, 0:width_x, width_y : 2 * width_y] = yhalo[begin : begin + width_x]
    xsend[0] = ext[:, width_x - 8 : width_x, :]
    xsend[1] = ext[:, 0:8, :]
    for place, step in enumerate((1, -1)):
        send(
            xsend.at[place],
            xbuf.at[place],
            x_send.at[place],
            x_recv.at[place],
            {"row": shifted(row, step, rows)},
        )

    for place in range(2):
        arrive(xbuf.at[place], x_send.at[place], x_recv.at[place], {"row": row})
    upper = lax.broadcasted_iota(jnp.int32, (2 * depth, 8, 2 * width_y), 1) < 4
    ext[:, width_x : width_x + 8, :] = jnp.where(upper, xbuf[1], xbuf[0])
    zsend[...] = ext[:, :, 0:width_y].reshape(zsend.shape).astype(jnp.bfloat16)
    margin = ext[:, :, width_y : 2 * width_y].reshape(zsend.shape).astype(jnp.bfloat16)
    blank = jnp.zeros((zcol.shape[1] - margin.shape[0], width_y), jnp.bfloat16)
    zcol[...] = lax.dot_general(
        pick,
        jnp.concatenate([margin, blank], axis=0),
        (((1,), (1,)), ((), ())),
        preferred_element_type=jnp.float32,
    )
    for place, step in enumerate((1, -1)):
        neighbour = {"col": shifted(col, step, cols)}
        send(zsend, zbuf.at[place], z_send.at[place], z_recv.at[place], neighbour)
        send(
            zcol, zcol_buf.at[place], z_send.at[2 + place], z_recv.at[2 + place], neighbour
        )
    shape = (2, depth, width_x + 8, 2 * width_y)
    field[:, depth : 2 * depth] = ext[...].reshape(shape)
    for plane in range(depth):
        pair = density_pair(labels_ref[plane], jitter_ref[0, plane], jitter_ref[1, plane])
        for part in range(2):
            field[part, depth + plane, 0:width_x, 0:width_y] = pair[part]

    lane = lax.broadcasted_iota(jnp.int32, (16, 128), 1)
    line_id = lax.broadcasted_iota(jnp.int32, (16, 256), 0)
    here = lax.broadcasted_iota(jnp.int32, (16, 256), 1) // 16 == line_id

    def spread(value):
        value = jnp.where(lane < 16, value, 0.0)
        for shift in (16, 32, 64):
            value = value + pltpu.roll(value, shift, 1)
        value = jnp.concatenate([value, value], axis=1)
        return jnp.sum(jnp.where(here, value, 0.0), axis=0, keepdims=True)

    def widen(value):
        blank = jnp.zeros((16, 128 - value.shape[1]), jnp.float32)
        return jnp.concatenate([value, blank], axis=1)

    def contract(left, right):
        return lax.dot_general(
            left, right, (((1,), (1,)), ((), ())), preferred_element_type=jnp.float32
        )

    @pl.when(hub)
    def _():
        arrive(shell_pair, s1_send.at[0], s1_recv.at[0], {"row": mirror})
        arrive(shell_next, s1_send.at[1], s1_recv.at[1], {"row": mirror})

        def joined(ref):
            return jnp.concatenate(
                [ref[source].astype(jnp.float32) for source in range(secs)], axis=1
            )

        mine, paired = joined(shell_rows), joined(shell_pair)
        minus = jnp.where(row < half, paired, mine)
        following = jnp.broadcast_to(joined(shell_next)[0:1], minus.shape)
        row_id = lax.broadcasted_iota(jnp.int32, minus.shape, 0)
        shells_all[0:width_x, :] = jnp.where(row < half, mine, paired)
        shells_all[width_x : 2 * width_x, :] = jnp.where(
            row_id == width_x - 1, following, pltpu.roll(minus, width_x - 1, 0)
        )
        tall = (16, full_y)
        label = lax.broadcasted_iota(jnp.int32, tall, 0).astype(jnp.float32)
        chunk = 8 * full_y

        def one_hot(digit):
            return jnp.where(jnp.broadcast_to(digit, tall) == label, 1.0, 0.0).astype(
                jnp.bfloat16
            )

        def build(step, total):
            value = shells_all[pl.ds(pl.multiple_of(step * 8, 8), 8), :]
            upper_digit = jnp.floor(value * (1.0 / 16.0))
            lower_digit = value - 16.0 * upper_digit
            begin = pl.multiple_of(step * chunk, chunk)
            for line in range(8):
                span = pl.ds(begin + line * full_y, full_y)
                mask_h[:, span] = one_hot(upper_digit[line : line + 1])
                mask_l[:, span] = one_hot(lower_digit[line : line + 1])
            span = pl.ds(begin, chunk)
            return total + contract(mask_h[:, span], mask_l[:, span])

        counts[...] = lax.fori_loop(
            0, 2 * width_x // 8, build, jnp.zeros((16, 16), jnp.float32)
        )

        ycopy.wait()
        half_buf[0] = half_send[...]
        for source in range(1, secs):
            arrive(
                half_buf.at[source], p2_send.at[0], p2_recv.at[source - 1], {"sec": sec}
            )
        left = jnp.concatenate([half_buf[source] for source in range(secs)], axis=1)
        product = jnp.dot(left, ytab[...], preferred_element_type=jnp.float32)
        re_cos, re_sin = product[:width_x, :full_y], product[:width_x, full_y:]
        im_cos, im_sin = product[width_x:, :full_y], product[width_x:, full_y:]
        first = (lax.broadcasted_iota(jnp.int32, (width_x, full_y), 0) == 0) & (block == 0)
        sum_re = jnp.where(first, re_cos, re_cos + im_sin)
        sum_im = jnp.where(first, re_sin, im_cos - re_sin)
        dif_re = jnp.where(first, im_cos, re_cos - im_sin)
        dif_im = jnp.where(first, im_sin, im_cos + re_sin)
        power[0] = sum_re * sum_re + sum_im * sum_im
        power[1] = dif_re * dif_re + dif_im * dif_im

        def gather(step, total):
            for sign in range(2):
                value = power[sign, pl.ds(pl.multiple_of(step * 8, 8), 8), :]
                coarse = value.astype(jnp.bfloat16).astype(jnp.float32)
                fine = value - coarse
                place = step if sign == 0 else 2 * width_x // 8 - 1 - step
                begin = pl.multiple_of(place * chunk, chunk)
                for line in range(8):
                    slot = line if sign == 0 else 7 - line
                    member = mask_l[:, pl.ds(begin + slot * full_y, full_y)]
                    span = slice(slot * full_y, (slot + 1) * full_y)
                    for half_id, part in enumerate((coarse, fine)):
                        line_value = jnp.broadcast_to(part[line : line + 1], tall)
                        weighted[sign, 16 * half_id : 16 * half_id + 16, span] = (
                            member * line_value.astype(jnp.bfloat16)
                        )
                total = total + contract(mask_h[:, pl.ds(begin, chunk)], weighted[sign])
            return total

        table = widen(
            lax.fori_loop(0, width_x // 8, gather, jnp.zeros((16, 32), jnp.float32))
        )
        row_send[0:1, :] = spread(table + pltpu.roll(table, 112, 1))
        row_send[1:2, :] = spread(widen(counts[...]))
        for step in order:
            transfer(
                row_send,
                row_buf.at[row],
                ar_send.at[step - 1],
                ar_recv.at[step - 1],
                {"row": shifted(row, step, rows)},
            ).start()
        row_buf[row] = row_send[...]

    for place, begin in enumerate((0, 2 * depth)):
        arrive(zbuf.at[place], z_send.at[place], z_recv.at[place], {"col": col})
        arrive(
            zcol_buf.at[place], z_send.at[2 + place], z_recv.at[2 + place], {"col": col}
        )
        side_shape = (2, depth, width_x + 8, width_y)
        margin = lax.dot_general(
            zcol_buf[place].T.astype(jnp.bfloat16),
            pick,
            (((1,), (0,)), ((), ())),
            preferred_element_type=jnp.float32,
        )[: zsend.shape[0]]
        field[:, begin : begin + depth, :, 0:width_y] = (
            zbuf[place].astype(jnp.float32).reshape(side_shape)
        )
        field[:, begin : begin + depth, :, width_y : 2 * width_y] = margin.reshape(side_shape)
    for part in range(2):
        populations_of(part, field, pop_ref)

    @pl.when(hub)
    def _():
        for step in order:
            arrive(
                row_buf.at[shifted(row, -step, rows)],
                ar_send.at[step - 1],
                ar_recv.at[step - 1],
                {"row": row},
            )
        sums = []
        for start in (0, half):
            total = row_buf[start]
            for source in range(start + 1, start + half):
                total = total + row_buf[source]
            sums.append(total)
        scale = sums[0][1:2] * float(full_x * full_y)
        spec_send[0:1, :] = sums[0][0:1] / scale
        spec_send[1:2, :] = sums[1][0:1] / scale
        spec_copies = [
            transfer(
                spec_send, spec_buf, as_send.at[target - 1], as_recv.at[0], {"sec": target}
            )
            for target in range(1, secs)
        ]
        for copy in spec_copies:
            copy.start()
        spec_ref[...] = spec_send[...]
        for copy in spec_copies:
            copy.wait_send()
        pair_copy.wait_send()

        @pl.when(row >= half)
        def _():
            for copy in next_copies:
                copy.wait_send()

        for step in order:
            transfer(
                row_send,
                row_buf.at[row],
                ar_send.at[step - 1],
                ar_recv.at[step - 1],
                {"row": row},
            ).wait_send()

    @pl.when(sec > 0)
    def _():
        arrive(spec_buf, as_send.at[0], as_recv.at[0], {"sec": sec})
        spec_ref[...] = spec_buf[...]
        ycopy.wait()
        shell_copy.wait_send()
        half_copy.wait_send()

    for copy in waits:
        copy.wait_send()


def exchange(labels, jitter, shells, sizes):
    rows, secs, _ = sizes
    depth, width_x, width_y = labels.shape
    full_x, full_y = width_x * rows, width_y * secs
    ext_rows = 2 * depth * (width_x + 8)
    col_lanes = -(-ext_rows // 128) * 128
    bf16, f32 = jnp.bfloat16, jnp.float32
    vmem = pl.BlockSpec(memory_space=pltpu.VMEM)
    hbm = pl.BlockSpec(memory_space=pl.ANY)
    dma = pltpu.SemaphoreType.DMA
    return pl.pallas_call(
        functools.partial(exchange_kernel, sizes),
        out_shape=(
            pltpu.VMEM((38, depth, width_x, width_y), f32),
            pltpu.VMEM((depth, NSHELL), f32),
        ),
        in_specs=[vmem, vmem, vmem, hbm, hbm],
        out_specs=(vmem, vmem),
        scratch_shapes=[
            pltpu.VMEM((2 * width_x, full_x), bf16),
            pltpu.VMEM((full_y, 2 * full_y), bf16),
            pltpu.VMEM((depth, width_x, width_y), bf16),
            pltpu.VMEM((rows, width_x, width_y), bf16),
            pltpu.VMEM((2 * width_x, width_y), bf16),
            pltpu.VMEM((secs, 2 * width_x, width_y), bf16),
            pltpu.VMEM((width_x, width_y), bf16),
            pltpu.VMEM((secs, width_x, width_y), bf16),
            pltpu.VMEM((secs, 16, width_y), bf16),
            pltpu.VMEM((secs, width_x, width_y), bf16),
            pltpu.VMEM((secs, 16, width_y), bf16),
            pltpu.VMEM((2 * width_x, full_y), f32),
            pltpu.VMEM((8, 2 * depth * width_x), f32),
            pltpu.VMEM((2, 8, 2 * depth * width_x), f32),
            pltpu.VMEM((2 * depth, width_x + 8, 2 * width_y), f32),
            pltpu.VMEM((2, 2 * depth, 8, 2 * width_y), f32),
            pltpu.VMEM((2, 2 * depth, 8, 2 * width_y), f32),
            pltpu.VMEM((ext_rows, width_y), bf16),
            pltpu.VMEM((2, ext_rows, width_y), bf16),
            pltpu.VMEM((8, col_lanes), f32),
            pltpu.VMEM((2, 8, col_lanes), f32),
            pltpu.VMEM((2, 3 * depth, width_x + 8, 2 * width_y), f32),
            pltpu.VMEM((16, 2 * width_x * full_y), bf16),
            pltpu.VMEM((16, 2 * width_x * full_y), bf16),
            pltpu.VMEM((2, 32, 8 * full_y), bf16),
            pltpu.VMEM((16, 16), f32),
            pltpu.VMEM((2, width_x, full_y), f32),
            pltpu.VMEM((2, NSHELL), f32),
            pltpu.VMEM((rows, 2, NSHELL), f32),
            pltpu.VMEM((2, NSHELL), f32),
            pltpu.VMEM((2, NSHELL), f32),
            dma((2,)),
            dma((rows - 1,)),
            dma((rows - 1,)),
            dma((1,)),
            dma((secs - 1,)),
            dma((3,)),
            dma((2,)),
            dma((1,)),
            dma((secs - 1,)),
            dma((2,)),
            dma((2,)),
            dma((2,)),
            dma((2,)),
            dma((4,)),
            dma((4,)),
            dma((rows - 1,)),
            dma((rows - 1,)),
            dma((secs - 1,)),
            dma((1,)),
        ],
        compiler_params=pltpu.CompilerParams(collective_id=0, has_side_effects=True),
        name="exchange",
    )(
        labels,
        jitter,
        shells,
        jnp.asarray(x_table(rows, width_x, full_x)),
        jnp.asarray(y_table(full_y)),
    )


def solution(mesh):
    sizes = tuple(mesh.shape[name] for name in ("row", "sec", "col"))

    def on_device(labels, jitter, shells):
        return exchange(labels, jitter, shells, sizes)

    in_specs = (P("col", "row", "sec"), P(None, "col", "row", "sec"), P("row", "sec"))
    out_specs = (P(None, "col", "row", "sec"), P("col", None))
    return jax.shard_map(
        on_device, mesh=mesh, in_specs=in_specs, out_specs=out_specs, check_vma=False
    )
```
